1024 devices in a mesh: seq: 16 (over y, core), dp: 64 (over x, z).
Axes of the slice: x: 8, y: 8, z: 8, core: 2. Of those that a mesh axis runs over, the one named last changes fastest.
Arguments:
- queries: bfloat16 [64, 2048, 512], P('dp', 'seq'), may hold values from -6 to 6
- keys: bfloat16 [64, 2048, 512], P('dp', 'seq'), may hold values from -6 to 6
- values: bfloat16 [64, 2048, 512], P('dp', 'seq'), may hold values from -6 to 6
- alpha: float32 [64, 2048, 4], P('dp', 'seq'), may hold values from -4 to 100000
- beta: float32 [64, 2048, 4], P('dp', 'seq'), may hold values from 0.05 to 0.2
- log_rate: float32 [4], replicated, may hold values from -12 to -3
- grad_out: bfloat16 [64, 2048, 512], P('dp', 'seq'), may hold values from -6 to 6
Outputs:
- outputs: bfloat16 [64, 2048, 512], P('dp', 'seq')
- grad_queries: bfloat16 [64, 2048, 512], P('dp', 'seq')
- grad_keys: bfloat16 [64, 2048, 512], P('dp', 'seq')
- grad_values: bfloat16 [64, 2048, 512], P('dp', 'seq')
- grad_alpha: float32 [64, 2048, 4], P('dp', 'seq')
- grad_beta: float32 [64, 2048, 4], P('dp', 'seq')
- grad_log_rate: float32 [4], replicated
The draws below stay inside these ranges and needn't reach their ends.
All inputs are finite; a program needn't handle non-finite values.
Results may differ from the reference program's by a relative error of at most 0.001.
Values sent between devices are 32-bit elements; how exact they have to be, the bound alone decides.
A program may use at most 64 MiB of HBM per device.

```python
import jax
import jax.numpy as jnp
from jax import lax

H = 4
DK = 128
DV = 128
BLOCK = 64
BATCH_ROWS = 64
SEQUENCE_LENGTH = 2048


def shared_draw(key):
    rate_key = jax.random.fold_in(key, 11)
    log_rate = jax.random.uniform(rate_key, (H,), jnp.float32, -12.0, -3.0)
    baseline_decay_gate = jnp.clip(jax.random.normal(jax.random.fold_in(key, 12), (BATCH_ROWS, SEQUENCE_LENGTH, H), jnp.float32), -4.0, 4.0)
    spike_locations = jax.random.randint(jax.random.fold_in(key, 13), (BATCH_ROWS, 2), 0, SEQUENCE_LENGTH)
    position_index = jnp.arange(SEQUENCE_LENGTH)
    spike_mask = jnp.any(position_index[None, :, None] == spike_locations[:, None, :], axis=-1)
    lost_share = jax.random.uniform(jax.random.fold_in(key, 16), (BATCH_ROWS, SEQUENCE_LENGTH, H), jnp.float32, 0.2, 0.5)
    expected_output = lost_share / jnp.exp(log_rate)[None, None, :]
    spike_decay_gate = expected_output + jnp.log(-jnp.expm1(-expected_output))
    alpha = jnp.where(spike_mask[..., None], jnp.maximum(spike_decay_gate, baseline_decay_gate), baseline_decay_gate)
    return (log_rate, alpha)


def draw_log_rate(key, part):
    return shared_draw(key)[0]


def draw_alpha(key, part):
    return shared_draw(key)[1]


def block_levels(rng, shape, split, least, high):
    gain = 1.0
    for axis_at, blocks in split:
        heights = jax.random.uniform(jax.random.fold_in(jax.random.fold_in(rng, 6), axis_at), (blocks,), jnp.float32, least / len(split), high / len(split))
        gain = gain * jnp.repeat(jnp.exp(heights), shape[axis_at] // blocks).reshape((-1,) + (1,) * (len(shape) - 1 - axis_at))
    return gain


def bell_draw(key, shape, scale, limit, shards=(), kind=jnp.bfloat16):
    loudness = block_levels(key, shape, shards, -0.22, 0.18) if shards else 1.0
    entries = jax.random.normal(key, shape, jnp.float32) * scale * loudness
    return jnp.minimum(jnp.maximum(entries, -limit), limit).astype(kind)


def setup_inputs(seed: int = 0) -> dict:
    arg_keys = jax.random.split(jax.random.key(seed), 8)
    queries = bell_draw(arg_keys[0], (BATCH_ROWS, SEQUENCE_LENGTH, H * DK), 1.0, 6.0, ((0, 64), (1, 16)))
    keys = bell_draw(arg_keys[1], (BATCH_ROWS, SEQUENCE_LENGTH, H * DK), 1.0, 6.0, ((0, 64), (1, 16)))
    values = bell_draw(arg_keys[2], (BATCH_ROWS, SEQUENCE_LENGTH, H * DV), 1.0, 6.0, ((0, 64), (1, 16)))
    alpha = draw_alpha(jax.random.fold_in(arg_keys[7], 71), 0)
    beta = jnp.clip(0.05 + 0.15 * jax.random.uniform(arg_keys[4], (BATCH_ROWS, SEQUENCE_LENGTH, H), jnp.float32) ** block_levels(arg_keys[4], (BATCH_ROWS, SEQUENCE_LENGTH, H), ((0, 64), (1, 16)), -0.2, 0.2), 0.05, 0.2)
    log_rate = draw_log_rate(jax.random.fold_in(arg_keys[7], 71), 0)
    grad_out = bell_draw(arg_keys[6], (BATCH_ROWS, SEQUENCE_LENGTH, H * DV), 1.0, 6.0, ((0, 64), (1, 16)))
    return dict(queries=queries, keys=keys, values=values, alpha=alpha, beta=beta, log_rate=log_rate, grad_out=grad_out)


EPSILON = 1e-06
highest = lax.Precision.HIGHEST

def to_blocks(tensor, blocks_count):
    moved = tensor.reshape((blocks_count, BLOCK) + tensor.shape[1:])
    return jnp.moveaxis(moved, 2, 0)

def recurrence(queries_n, keys_n, values_n, log_gate, betas, initial, with_output):
    length = keys_n.shape[0]
    blocks_count = length // BLOCK
    query_b = to_blocks(queries_n, blocks_count)
    key_b = to_blocks(keys_n, blocks_count)
    value_b = to_blocks(values_n, blocks_count)
    gate_b = to_blocks(log_gate, blocks_count)
    beta_b = to_blocks(betas, blocks_count)
    cumulated = jnp.cumsum(gate_b, axis=-1)
    spread = cumulated[..., :, None] - cumulated[..., None, :]
    row_ids = lax.broadcasted_iota(jnp.int32, (BLOCK, BLOCK), 0)
    col_ids = lax.broadcasted_iota(jnp.int32, (BLOCK, BLOCK), 1)
    inside = jnp.exp(jnp.where(row_ids >= col_ids, spread, -jnp.inf))
    strictly = jnp.where(row_ids > col_ids, inside, 0.0)
    key_gram = jnp.einsum('hncd,hnsd->hncs', key_b, key_b, precision=highest)
    system = jnp.eye(BLOCK, dtype=key_b.dtype) + beta_b[..., None] * strictly * key_gram
    decayed = jnp.exp(cumulated)
    value_part = jax.scipy.linalg.solve_triangular(system, beta_b[..., None] * value_b, lower=True, unit_diagonal=True)
    key_part = jax.scipy.linalg.solve_triangular(system, (beta_b * decayed)[..., None] * key_b, lower=True, unit_diagonal=True)
    to_end = jnp.exp(cumulated[..., -1:] - cumulated)
    key_end = key_b * to_end[..., None]
    block_decay = decayed[..., -1]
    sequence = [value_part, key_part, key_end, block_decay]
    if with_output:
        query_scores = jnp.einsum('hncd,hnsd->hncs', query_b, key_b, precision=highest) * inside
        sequence = sequence + [query_b * decayed[..., None], query_scores]
    moved_in = [jnp.moveaxis(member, 1, 0) for member in sequence]

    def advance(carried, inputs):
        correction = inputs[0] - jnp.einsum('hcd,hde->hce', inputs[1], carried, precision=highest)
        updated = inputs[3][:, None, None] * carried + jnp.einsum('hcd,hce->hde', inputs[2], correction, precision=highest)
        if with_output:
            emitted = jnp.einsum('hcd,hde->hce', inputs[4], carried, precision=highest)
            emitted = emitted + jnp.einsum('hcs,hse->hce', inputs[5], correction, precision=highest)
            return (updated, emitted)
        return (updated, jnp.zeros((), carried.dtype))
    final_state, emitted = lax.scan(advance, initial, moved_in)
    if not with_output:
        return (None, final_state)
    head_count = emitted.shape[1]
    value_width = emitted.shape[3]
    result = jnp.transpose(emitted, (0, 2, 1, 3)).reshape(length, head_count * value_width)
    return (result, final_state)

def prepared(query_f, key_f, alpha_f, log_rate):
    length = query_f.shape[0]

    def normalize(tensor):
        shaped = tensor.reshape(length, H, DK)
        return shaped * lax.rsqrt(lax.optimization_barrier(jnp.sum(shaped * shaped, axis=-1, keepdims=True)) + EPSILON)
    log_gate = -jnp.exp(log_rate)[None, :] * jax.nn.softplus(alpha_f)
    return (normalize(query_f), normalize(key_f), log_gate)

def layer(query_f, key_f, value_f, alpha_f, beta_f, log_rate, initial):
    length = query_f.shape[0]
    queries_n, keys_n, log_gate = prepared(query_f, key_f, alpha_f, log_rate)
    return recurrence(queries_n, keys_n, value_f.reshape(length, H, DV), log_gate, beta_f, initial, True)

def reference(queries, keys, values, alpha, beta, log_rate, grad_out):

    def per_sequence(members):
        query_in, key_in, value_in, alpha_in, beta_in, cotangent = members
        initial = jnp.zeros((H, DK, DV), jnp.float32)

        def forward(query_f, key_f, value_f, alpha_f, beta_f, rate_f):
            return layer(query_f, key_f, value_f, alpha_f, beta_f, rate_f, initial)[0]
        result, pullback = jax.vjp(forward, query_in.astype(jnp.float32), key_in.astype(jnp.float32), value_in.astype(jnp.float32), alpha_in, beta_in, log_rate)
        gradients = pullback(cotangent.astype(jnp.float32))
        return (result.astype(jnp.bfloat16), gradients[0].astype(jnp.bfloat16), gradients[1].astype(jnp.bfloat16), gradients[2].astype(jnp.bfloat16), gradients[3], gradients[4], gradients[5])
    mapped = lax.map(per_sequence, (queries, keys, values, alpha, beta, grad_out))
    return (mapped[0], mapped[1], mapped[2], mapped[3], mapped[4], mapped[5], lax.optimization_barrier(jnp.sum(mapped[6], axis=0)))
```

```python
import functools

import jax
import jax.numpy as jnp
from jax import lax
from jax.experimental import pallas as pl
from jax.experimental.pallas import tpu as pltpu
from jax.sharding import Mesh
from jax.sharding import PartitionSpec as P

H = 4
D = 128
C = 128
EPSILON = 1e-06
ROWS = 32
MESH = pl.DeviceIdType.MESH
f32 = jnp.float32
bf16 = jnp.bfloat16


def mm(a, b):
    return lax.dot_general(a, b, (((1,), (0,)), ((), ())), preferred_element_type=f32)


def mm_t(a, b):
    return lax.dot_general(a, b, (((1,), (1,)), ((), ())), preferred_element_type=f32)


def split(x):
    high = x.astype(bf16)
    return high, (x - high.astype(f32)).astype(bf16)


def split3(x):
    high, rest = x.astype(bf16), None
    rest = x - high.astype(f32)
    mid = rest.astype(bf16)
    return high, mid, (rest - mid.astype(f32)).astype(bf16)


def wide(x):
    return jnp.concatenate(split(x), axis=1)


def tall2(x):
    return jnp.concatenate([x, x], axis=0)


def fold(x):
    half = x.shape[1] // 2
    return x[:, :half] + x[:, half:]


def right(b):
    return tall2(wide(b))


def right_t(b):
    high, low = split(b)
    return jnp.concatenate(
        [jnp.concatenate([high, high], axis=1), jnp.concatenate([low, low], axis=1)], axis=0
    )


def rows_of(x):
    return jnp.sum(x, axis=1, keepdims=True)


def kernel(
    sizes,
    q_ref, k_ref, v_ref, alpha_ref, beta_ref, rate_ref, do_ref,
    o_ref, dq_ref, dk_ref, dv_ref, dalpha_ref, dbeta_ref, drate_ref,
    tbc, exch, chip_t, chip_tt, chip_b, chip_c,
    fin, fout, bin_, bout, sends, sendd, s0, ds1,
    keep_u, keep_pu, keep_y0, keep_ew, keep_f1,
    ar_seq, ar_x, ar_z, ar_own,
    exch_send, exch_recv, f_send, f_recv, b_send, b_recv, s_send, s_recv, d_send, d_recv,
    seq_send, seq_recv, x_send, x_recv, z_send, z_recv,
):
    ny, nx, nz = sizes
    y = lax.axis_index("y")
    c = lax.axis_index("c")
    ix = lax.axis_index("x")
    iz = lax.axis_index("z")
    nseq = 2 * ny
    me = 2 * y + c
    other = 1 - c

    barrier = pltpu.get_barrier_semaphore()
    for step in range(1, nseq):
        peer = lax.rem(me + step, nseq)
        pl.semaphore_signal(barrier, inc=1, device_id={"y": peer // 2, "c": lax.rem(peer, 2)}, device_id_type=MESH)
    for step in range(1, nx):
        pl.semaphore_signal(barrier, inc=1, device_id={"x": lax.rem(ix + step, nx)}, device_id_type=MESH)
    for step in range(1, nz):
        pl.semaphore_signal(barrier, inc=1, device_id={"z": lax.rem(iz + step, nz)}, device_id_type=MESH)

    heads = range(H)
    row = lax.broadcasted_iota(jnp.int32, (C, C), 0)
    col = lax.broadcasted_iota(jnp.int32, (C, C), 1)
    lower = row >= col
    strict = row > col
    upper = row <= col
    strict_upper = row < col
    eye = jnp.where(row == col, 1.0, 0.0).astype(f32)

    def part(ref, h):
        return ref[:, h * D:(h + 1) * D]

    alpha = alpha_ref[...]
    beta = beta_ref[...]
    head_row = lax.broadcasted_iota(jnp.int32, (H, C), 0)
    rate = jnp.zeros((H, C), f32)
    for h in heads:
        rate = jnp.where(head_row == h, rate_ref[h], rate)
    rate = jnp.exp(rate)
    soft = jnp.maximum(alpha, 0.0) + jnp.log1p(jnp.exp(-jnp.abs(alpha)))
    log_gate = -rate * soft
    bounded = jnp.maximum(log_gate, -120.0)
    tri_up = jnp.where(upper, 1.0, 0.0).astype(bf16)
    summed = mm(jnp.concatenate(split3(bounded), axis=0), tri_up)
    g_rows = summed[:H] + summed[H:2 * H] + summed[2 * H:]
    stacked = jnp.concatenate([g_rows, beta], axis=0)
    columns = jnp.transpose(jnp.concatenate([stacked, jnp.zeros((C - 2 * H, C), f32)], axis=0))

    g_r = [g_rows[h:h + 1, :] for h in heads]
    b_r = [beta[h:h + 1, :] for h in heads]
    g_c = [columns[:, h:h + 1] for h in heads]
    b_c = [columns[:, H + h:H + h + 1] for h in heads]
    g_end = [g_rows[h:h + 1, C - 1:C] for h in heads]
    gamma = [jnp.exp(g_end[h]) for h in heads]
    grow_c = [jnp.exp(g_c[h]) for h in heads]
    grow_r = [jnp.exp(g_r[h]) for h in heads]
    end_c = [jnp.exp(g_end[h] - g_c[h]) for h in heads]

    gram = []
    for h in heads:
        both = jnp.concatenate([part(k_ref, h), part(q_ref, h)], axis=0)
        gram.append(mm_t(both, both))
    rk_c, rk_r, rq_c, rq_r = [], [], [], []
    for h in heads:
        kk = gram[h][:C, :C] * eye
        qq = gram[h][C:, C:] * eye
        rk_c.append(lax.rsqrt(rows_of(kk) + EPSILON))
        rk_r.append(lax.rsqrt(jnp.sum(kk, axis=0, keepdims=True) + EPSILON))
        rq_c.append(lax.rsqrt(rows_of(qq) + EPSILON))
        rq_r.append(lax.rsqrt(jnp.sum(qq, axis=0, keepdims=True) + EPSILON))

    def decay(h):
        return jnp.exp(jnp.where(lower, g_c[h] - g_r[h], -1e30))

    def decay_t(h):
        return jnp.exp(jnp.where(upper, g_r[h] - g_c[h], -1e30))

    a_mat, p_mat, pt_mat = [], [], []
    for h in heads:
        fall = decay(h)
        scaled = fall * rk_r[h]
        a_mat.append(jnp.where(strict, gram[h][:C, :C] * scaled * (b_c[h] * rk_c[h]), 0.0))
        p_mat.append(gram[h][C:, :C] * scaled * rq_c[h])
        pt_mat.append(gram[h][:C, C:] * (decay_t(h) * rq_r[h]) * rk_c[h])

    same16 = (row // 16) == (col // 16)
    same64 = (row // 64) == (col // 64)
    power, inv = [], []
    for h in heads:
        a16 = jnp.where(same16, a_mat[h], 0.0)
        inv.append(eye - a16)
        power.append(fold(mm(wide(a16), right(a16))))
    for level in range(2):
        for h in heads:
            both = fold(mm(jnp.concatenate([wide(inv[h]), wide(power[h])], axis=0), right(power[h])))
            inv[h] = inv[h] + both[:C]
            power[h] = both[C:]
    for h in heads:
        inv[h] = inv[h] + fold(mm(wide(inv[h]), right(power[h])))
    step_mat = []
    for h in heads:
        off = jnp.where(same64, jnp.where(same16, 0.0, a_mat[h]), 0.0)
        step_mat.append(fold(mm(wide(inv[h]), right(off))))
    square = []
    for h in heads:
        both = mm(wide(step_mat[h]), jnp.concatenate([right(inv[h]), right(step_mat[h])], axis=1))
        inv[h] = inv[h] - fold(both[:, :2 * C])
        square.append(fold(both[:, 2 * C:]))
    for h in heads:
        inv[h] = inv[h] + fold(mm(wide(square[h]), right(inv[h])))
    for h in heads:
        off = jnp.where(same64, 0.0, a_mat[h])
        step_mat[h] = fold(mm(wide(inv[h]), right(off)))
    for h in heads:
        inv[h] = inv[h] - fold(mm(wide(step_mat[h]), right(inv[h])))

    u_mat, w_mat = [], []
    for h in heads:
        key, value = part(k_ref, h), part(v_ref, h)
        u_mat.append(mm(wide(inv[h] * b_r[h]), tall2(value)))
        w_mat.append(mm(wide(inv[h] * (b_r[h] * grow_r[h] * rk_r[h])), tall2(key)))
    for h in heads:
        scale = end_c[h] * rk_c[h]
        key_t = jnp.transpose(part(k_ref, h))
        tb = mm(key_t, jnp.concatenate([wide(w_mat[h] * scale), wide(u_mat[h] * scale)], axis=1))
        tbc[h, 0] = gamma[h] * eye - fold(tb[:, :2 * D])
        tbc[h, 1] = jnp.transpose(fold(tb[:, 2 * D:]))
    for h in heads:
        pwu = mm(wide(p_mat[h]), jnp.concatenate([right(w_mat[h]), right(u_mat[h])], axis=1))
        keep_pu[h] = fold(pwu[:, 2 * D:])
        keep_u[h] = u_mat[h]
        e1 = part(q_ref, h).astype(f32) * (rq_c[h] * grow_c[h]) - fold(pwu[:, :2 * D])
        keep_ew[h, :C] = wide(e1)
        keep_ew[h, C:] = wide(w_mat[h])
        tbc[h, 2] = fold(mm(jnp.transpose(part(do_ref, h)), wide(e1)))

    pl.semaphore_wait(barrier, nseq - 1 + nx - 1 + nz - 1)

    def swap(hh):
        return pltpu.make_async_remote_copy(
            src_ref=tbc.at[2 * other + hh], dst_ref=exch.at[hh],
            send_sem=exch_send.at[hh], recv_sem=exch_recv.at[hh],
            device_id={"c": other}, device_id_type=MESH,
        )

    for hh in range(2):
        swap(hh).start()

    for h in heads:
        z = mm(wide(pt_mat[h]), tall2(part(do_ref, h)))
        inv_t = wide(jnp.transpose(inv[h]))
        key_end = part(k_ref, h).astype(f32) * (end_c[h] * rk_c[h])
        both = mm(inv_t, jnp.concatenate([right(z), right(key_end)], axis=1))
        keep_y0[h] = fold(both[:, :2 * D])
        keep_f1[h] = wide(fold(both[:, 2 * D:]))

    first = c == 0
    for hh in range(2):
        swap(hh).wait()

    def pair(hh, item):
        mine, theirs = tbc[2 * c + hh, item], exch[hh, item]
        return jnp.where(first, mine, theirs), jnp.where(first, theirs, mine)

    for hh in range(2):
        t0, t1 = pair(hh, 0)
        b0, b1 = pair(hh, 1)
        c0, c1 = pair(hh, 2)
        both = fold(mm(jnp.concatenate([wide(t1), wide(c1)], axis=0), right(t0)))
        whole = both[:D]
        chip_t[hh] = right(whole)
        chip_tt[hh] = right_t(whole)
        chip_b[hh] = fold(mm_t(wide(b0), right_t(t1))) + b1
        chip_c[hh] = both[D:] + c0

    chunks = [(hh, r) for hh in range(2) for r in range(0, D, ROWS)]

    def f_copy(i, source):
        hh, r = chunks[i]
        return pltpu.make_async_remote_copy(
            src_ref=source.at[hh, pl.ds(r, ROWS)], dst_ref=fin.at[hh, pl.ds(r, ROWS)],
            send_sem=f_send.at[i], recv_sem=f_recv.at[i],
            device_id={"y": lax.rem(y + 1, ny)}, device_id_type=MESH,
        )

    def b_copy(i, source):
        hh, r = chunks[i]
        return pltpu.make_async_remote_copy(
            src_ref=source.at[hh, pl.ds(r, ROWS)], dst_ref=bin_.at[hh, pl.ds(r, ROWS)],
            send_sem=b_send.at[i], recv_sem=b_recv.at[i],
            device_id={"y": lax.rem(y + ny - 1, ny)}, device_id_type=MESH,
        )

    def s_copy(hh):
        return pltpu.make_async_remote_copy(
            src_ref=sends.at[hh], dst_ref=s0.at[2 * c + hh],
            send_sem=s_send.at[hh], recv_sem=s_recv.at[hh],
            device_id={"c": other}, device_id_type=MESH,
        )

    def d_copy(hh):
        return pltpu.make_async_remote_copy(
            src_ref=sendd.at[hh], dst_ref=ds1.at[2 * c + hh],
            send_sem=d_send.at[hh], recv_sem=d_recv.at[hh],
            device_id={"c": other}, device_id_type=MESH,
        )

    def forward():
        @pl.when(y == 0)
        def _():
            for i in range(len(chunks)):
                f_copy(i, chip_b).start()
            fin[...] = jnp.zeros_like(fin)

        @pl.when(y > 0)
        def _():
            for i, (hh, r) in enumerate(chunks):
                f_copy(i, fout).wait_recv()

                @pl.when(y < ny - 1)
                def _():
                    here = pl.ds(r, ROWS)
                    fout[hh, here] = fold(mm_t(wide(fin[hh, here]), chip_tt[hh])) + chip_b[hh, here]
                    f_copy(i, fout).start()

        for hh in range(2):
            t0, _ = pair(hh, 0)
            b0, _ = pair(hh, 1)
            start = fin[hh]
            middle = fold(mm_t(wide(start), right_t(t0))) + b0
            s0[2 * c + hh] = jnp.where(first, start, middle)
            sends[hh] = jnp.where(first, middle, start)
            s_copy(hh).start()

    def backward():
        @pl.when(y == ny - 1)
        def _():
            for i in range(len(chunks)):
                b_copy(i, chip_c).start()
            bin_[...] = jnp.zeros_like(bin_)

        @pl.when(y < ny - 1)
        def _():
            for i, (hh, r) in enumerate(chunks):
                b_copy(i, bout).wait_recv()

                @pl.when(y > 0)
                def _():
                    here = pl.ds(r, ROWS)
                    bout[hh, here] = fold(mm(wide(bin_[hh, here]), chip_t[hh])) + chip_c[hh, here]
                    b_copy(i, bout).start()

        for hh in range(2):
            _, t1 = pair(hh, 0)
            _, c1 = pair(hh, 2)
            end = bin_[hh]
            middle = fold(mm(wide(end), right(t1))) + c1
            ds1[2 * c + hh] = jnp.where(first, middle, end)
            sendd[hh] = jnp.where(first, end, middle)
            d_copy(hh).start()

    @pl.when(y < ny // 2)
    def _():
        forward()
        backward()

    @pl.when(y >= ny // 2)
    def _():
        backward()
        forward()

    for hh in range(2):
        s_copy(hh).wait()
        d_copy(hh).wait()

    @pl.when(y < ny - 1)
    def _():
        for i in range(len(chunks)):
            f_copy(i, fout).wait_send()

    @pl.when(y > 0)
    def _():
        for i in range(len(chunks)):
            b_copy(i, bout).wait_send()

    d_mat, y_mat, start_w, end_w, dot_s = [], [], [], [], []
    for h in heads:
        start, end = s0[h], ds1[h]
        start_w.append(start)
        end_w.append(end)
        dot_s.append(jnp.sum(jnp.sum(start * end, axis=0, keepdims=True), axis=1, keepdims=True))
        ew = fold(mm_t(keep_ew[h], right_t(start)))
        o_ref[:, h * D:(h + 1) * D] = (keep_pu[h] + ew[:C]).astype(bf16)
        d_mat.append(keep_u[h] - ew[C:])
        y_mat.append(keep_y0[h] + fold(mm_t(keep_f1[h], right_t(end))))
    lane = lax.broadcasted_iota(jnp.int32, (C, C), 1)
    gathered = jnp.zeros((C, C), f32)
    last = lax.broadcasted_iota(jnp.int32, (C, 1), 0) == C - 1
    for h in heads:
        key, query, value, cot = part(k_ref, h), part(q_ref, h), part(v_ref, h), part(do_ref, h)
        dm, ym = d_mat[h], y_mat[h]
        left = jnp.concatenate([jnp.concatenate([cot, jnp.zeros_like(cot)], axis=1), wide(ym)], axis=0)
        with_s = fold(mm(left, right(start_w[h])))
        with_d = fold(mm_t(left, right_t(dm)))
        y_high, y_low = split(ym)
        flipped = mm_t(
            wide(dm),
            jnp.concatenate([
                jnp.concatenate([cot, cot], axis=1),
                jnp.concatenate([y_high, y_high], axis=1),
                jnp.concatenate([y_low, y_low], axis=1),
            ], axis=0),
        )
        dds = fold(mm(wide(dm), right(end_w[h]))) * end_c[h]
        fall = decay(h) * rk_r[h]
        fall_t = decay_t(h)
        x_w = with_d[:C] * fall
        n_w = jnp.where(strict, with_d[C:] * fall, 0.0) * (-b_c[h])
        xn = mm(jnp.concatenate([wide(x_w), wide(n_w)], axis=0), tall2(key))
        xt = flipped[:, :C] * (fall_t * rq_r[h])
        nt = jnp.where(strict_upper, (flipped[:, C:2 * C] + flipped[:, 2 * C:]) * fall_t, 0.0) * (-b_r[h] * rk_r[h])
        dk_col = mm(jnp.concatenate([wide(nt), wide(xt)], axis=1), jnp.concatenate([tall2(key), tall2(query)], axis=0)) + dds
        dqn = with_s[:C] * grow_c[h] + xn[:C]
        dk_row = xn[C:] - with_s[C:] * (b_c[h] * grow_c[h])
        kn = key.astype(f32) * rk_c[h]
        qn = query.astype(f32) * rq_c[h]
        sum_q = rows_of(qn * dqn)
        sum_r = rows_of(kn * dk_row)
        sum_c = rows_of(kn * dk_col)
        sum_e = jnp.sum(rows_of(kn * dds), axis=0, keepdims=True)
        sum_v = rows_of(ym * value.astype(f32))
        dq_ref[:, h * D:(h + 1) * D] = ((dqn - qn * sum_q) * rq_c[h]).astype(bf16)
        dk_ref[:, h * D:(h + 1) * D] = ((dk_row + dk_col - kn * (sum_r + sum_c)) * rk_c[h]).astype(bf16)
        dv_ref[:, h * D:(h + 1) * D] = (ym * b_c[h]).astype(bf16)
        dbeta = sum_v + sum_r / b_c[h]
        dg = sum_q + sum_r - sum_c + jnp.where(last, sum_e + gamma[h] * dot_s[h], 0.0)
        gathered = jnp.where(lane == h, dg, gathered)
        gathered = jnp.where(lane == H + h, dbeta, gathered)
    as_rows = jnp.transpose(gathered)
    dbeta_ref[...] = as_rows[H:2 * H]
    tri_low = jnp.where(lower, 1.0, 0.0).astype(bf16)
    back = mm(jnp.concatenate(split3(as_rows[:H]), axis=0), tri_low)
    dlog = back[:H] + back[H:2 * H] + back[2 * H:]
    dalpha_ref[...] = dlog * -rate * jax.nn.sigmoid(alpha)
    own = jnp.concatenate([dlog * log_gate, jnp.zeros((8 - H, C), f32)], axis=0)

    def stage(total, slot, count, buf, send, recv, device):
        ar_own[slot] = total
        if count == 1:
            return total
        index = {0: me, 1: ix, 2: iz}[slot]

        def copy(step):
            return pltpu.make_async_remote_copy(
                src_ref=ar_own.at[slot], dst_ref=buf.at[index],
                send_sem=send.at[step], recv_sem=recv.at[step],
                device_id=device(lax.rem(index + step, count)), device_id_type=MESH,
            )

        for step in range(1, count):
            copy(step).start()
        buf[index] = total
        for step in range(1, count):
            copy(step).wait()
        result = buf[0]
        for j in range(1, count):
            result = result + buf[j]
        return result

    total = stage(own, 0, nseq, ar_seq, seq_send, seq_recv, lambda p: {"y": p // 2, "c": lax.rem(p, 2)})
    total = stage(total, 1, nx, ar_x, x_send, x_recv, lambda p: {"x": p})
    total = stage(total, 2, nz, ar_z, z_send, z_recv, lambda p: {"z": p})
    for h in heads:
        drate_ref[h] = jnp.sum(total[h:h + 1, :])


def local(sizes, queries, keys, values, alpha, beta, log_rate, grad_out):
    ny, nx, nz = sizes
    vmem = pl.BlockSpec(memory_space=pltpu.VMEM)
    smem = pl.BlockSpec(memory_space=pltpu.SMEM)
    wide_out = jax.ShapeDtypeStruct((C, H * D), bf16)
    gate_out = jax.ShapeDtypeStruct((H, C), f32)
    chunk_count = 2 * (D // ROWS)
    dma = pltpu.SemaphoreType.DMA
    square = (D, D)
    outs = pl.pallas_call(
        functools.partial(kernel, sizes),
        name="delta_rule",
        out_shape=(wide_out, wide_out, wide_out, wide_out, gate_out, gate_out, jax.ShapeDtypeStruct((H,), f32)),
        in_specs=[vmem, vmem, vmem, vmem, vmem, smem, vmem],
        out_specs=(vmem, vmem, vmem, vmem, vmem, vmem, smem),
        scratch_shapes=[
            pltpu.VMEM((H, 3) + square, f32),
            pltpu.VMEM((2, 3) + square, f32),
            pltpu.VMEM((2, 2 * D, 2 * D), bf16),
            pltpu.VMEM((2, 2 * D, 2 * D), bf16),
            pltpu.VMEM((2,) + square, f32),
            pltpu.VMEM((2,) + square, f32),
            pltpu.VMEM((2,) + square, f32),
            pltpu.VMEM((2,) + square, f32),
            pltpu.VMEM((2,) + square, f32),
            pltpu.VMEM((2,) + square, f32),
            pltpu.VMEM((2,) + square, f32),
            pltpu.VMEM((2,) + square, f32),
            pltpu.VMEM((H,) + square, f32),
            pltpu.VMEM((H,) + square, f32),
            pltpu.VMEM((H,) + square, f32),
            pltpu.VMEM((H,) + square, f32),
            pltpu.VMEM((H,) + square, f32),
            pltpu.VMEM((H, 2 * C, 2 * D), bf16),
            pltpu.VMEM((H, C, 2 * D), bf16),
            pltpu.VMEM((2 * ny, 8, C), f32),
            pltpu.VMEM((nx, 8, C), f32),
            pltpu.VMEM((nz, 8, C), f32),
            pltpu.VMEM((3, 8, C), f32),
            dma((2,)), dma((2,)),
            dma((chunk_count,)), dma((chunk_count,)),
            dma((chunk_count,)), dma((chunk_count,)),
            dma((2,)), dma((2,)), dma((2,)), dma((2,)),
            dma((2 * ny,)), dma((2 * ny,)),
            dma((nx,)), dma((nx,)), dma((nz,)), dma((nz,)),
        ],
        compiler_params=pltpu.CompilerParams(collective_id=0, has_side_effects=True),
    )(
        queries[0], keys[0], values[0],
        jnp.swapaxes(alpha[0], 0, 1), jnp.swapaxes(beta[0], 0, 1), log_rate, grad_out[0],
    )
    return (
        outs[0][None], outs[1][None], outs[2][None], outs[3][None],
        jnp.swapaxes(outs[4], 0, 1)[None], jnp.swapaxes(outs[5], 0, 1)[None], outs[6],
    )


def build(devices, ny, nx, nz):
    axes = Mesh(devices.reshape(ny, 2, nx, nz), ("y", "c", "x", "z"))
    rows = P(("x", "z"), ("y", "c"), None)
    return jax.shard_map(
        functools.partial(local, (ny, nx, nz)),
        mesh=axes,
        in_specs=(rows, rows, rows, rows, rows, P(), rows),
        out_specs=(rows, rows, rows, rows, rows, rows, P()),
        check_vma=False,
    )


def solution(mesh):
    return build(mesh.devices, 8, 8, 8)
```

```python
import functools

import jax
import jax.numpy as jnp
from jax import lax
from jax.experimental import pallas as pl
from jax.experimental.pallas import tpu as pltpu
from jax.sharding import Mesh
from jax.sharding import PartitionSpec as P

H = 4
D = 128
C = 128
EPSILON = 1e-06
ROWS = 32
MESH = pl.DeviceIdType.MESH
f32 = jnp.float32
bf16 = jnp.bfloat16


def mm(a, b):
    return lax.dot_general(a, b, (((1,), (0,)), ((), ())), preferred_element_type=f32)


def mm_t(a, b):
    return lax.dot_general(a, b, (((1,), (1,)), ((), ())), preferred_element_type=f32)


def split(x):
    high = x.astype(bf16)
    return high, (x - high.astype(f32)).astype(bf16)


def split3(x):
    high, rest = x.astype(bf16), None
    rest = x - high.astype(f32)
    mid = rest.astype(bf16)
    return high, mid, (rest - mid.astype(f32)).astype(bf16)


def wide(x):
    return jnp.concatenate(split(x), axis=1)


def tall2(x):
    return jnp.concatenate([x, x], axis=0)


def fold(x):
    half = x.shape[1] // 2
    return x[:, :half] + x[:, half:]


def right(b):
    return tall2(wide(b))


def right_t(b):
    high, low = split(b)
    return jnp.concatenate(
        [jnp.concatenate([high, high], axis=1), jnp.concatenate([low, low], axis=1)], axis=0
    )


def rows_of(x):
    return jnp.sum(x, axis=1, keepdims=True)


def kernel(
    sizes,
    q_ref, k_ref, v_ref, alpha_ref, beta_ref, rate_ref, do_ref,
    o_ref, dq_ref, dk_ref, dv_ref, dalpha_ref, dbeta_ref, drate_ref,
    tbc, exch, chip_t, chip_tt, chip_b, chip_c,
    fin, fout, bin_, bout, sends, sendd, s0, ds1,
    keep_u, keep_pu, keep_y0, keep_ew, keep_f1, keep_pa,
    ar_seq, ar_x, ar_z, ar_own,
    exch_send, exch_recv, f_send, f_recv, b_send, b_recv, s_send, s_recv, d_send, d_recv,
    seq_send, seq_recv, x_send, x_recv, z_send, z_recv,
):
    ny, nx, nz = sizes
    y = lax.axis_index("y")
    c = lax.axis_index("c")
    ix = lax.axis_index("x")
    iz = lax.axis_index("z")
    nseq = 2 * ny
    me = 2 * y + c
    other = 1 - c

    barrier = pltpu.get_barrier_semaphore()
    for step in range(1, nseq):
        peer = lax.rem(me + step, nseq)
        pl.semaphore_signal(barrier, inc=1, device_id={"y": peer // 2, "c": lax.rem(peer, 2)}, device_id_type=MESH)
    for step in range(1, nx):
        pl.semaphore_signal(barrier, inc=1, device_id={"x": lax.rem(ix + step, nx)}, device_id_type=MESH)
    for step in range(1, nz):
        pl.semaphore_signal(barrier, inc=1, device_id={"z": lax.rem(iz + step, nz)}, device_id_type=MESH)

    heads = range(H)
    row = lax.broadcasted_iota(jnp.int32, (C, C), 0)
    col = lax.broadcasted_iota(jnp.int32, (C, C), 1)
    lower = row >= col
    strict = row > col
    upper = row <= col
    strict_upper = row < col
    eye = jnp.where(row == col, 1.0, 0.0).astype(f32)

    def part(ref, h):
        return ref[:, h * D:(h + 1) * D]

    alpha = alpha_ref[...]
    beta = beta_ref[...]
    head_row = lax.broadcasted_iota(jnp.int32, (H, C), 0)
    rate = jnp.zeros((H, C), f32)
    for h in heads:
        rate = jnp.where(head_row == h, rate_ref[h], rate)
    rate = jnp.exp(rate)
    soft = jnp.maximum(alpha, 0.0) + jnp.log1p(jnp.exp(-jnp.abs(alpha)))
    log_gate = -rate * soft
    bounded = jnp.maximum(log_gate, -120.0)
    tri_up = jnp.where(upper, 1.0, 0.0).astype(bf16)
    summed = mm(jnp.concatenate(split3(bounded), axis=0), tri_up)
    g_rows = summed[:H] + summed[H:2 * H] + summed[2 * H:]
    stacked = jnp.concatenate([g_rows, beta], axis=0)
    columns = jnp.transpose(jnp.concatenate([stacked, jnp.zeros((C - 2 * H, C), f32)], axis=0))

    g_r = [g_rows[h:h + 1, :] for h in heads]
    b_r = [beta[h:h + 1, :] for h in heads]
    g_c = [columns[:, h:h + 1] for h in heads]
    b_c = [columns[:, H + h:H + h + 1] for h in heads]
    g_end = [g_rows[h:h + 1, C - 1:C] for h in heads]
    gamma = [jnp.exp(g_end[h]) for h in heads]
    grow_c = [jnp.exp(g_c[h]) for h in heads]
    grow_r = [jnp.exp(g_r[h]) for h in heads]
    end_c = [jnp.exp(g_end[h] - g_c[h]) for h in heads]

    gram = []
    for h in heads:
        both = jnp.concatenate([part(k_ref, h), part(q_ref, h)], axis=0)
        gram.append(mm_t(both, both))
    rk_c, rk_r, rq_c, rq_r = [], [], [], []
    for h in heads:
        kk = gram[h][:C, :C] * eye
        qq = gram[h][C:, C:] * eye
        rk_c.append(lax.rsqrt(rows_of(kk) + EPSILON))
        rk_r.append(lax.rsqrt(jnp.sum(kk, axis=0, keepdims=True) + EPSILON))
        rq_c.append(lax.rsqrt(rows_of(qq) + EPSILON))
        rq_r.append(lax.rsqrt(jnp.sum(qq, axis=0, keepdims=True) + EPSILON))

    def decay(h):
        return jnp.exp(jnp.where(lower, g_c[h] - g_r[h], -1e30))

    def decay_t(h):
        return jnp.exp(jnp.where(upper, g_r[h] - g_c[h], -1e30))

    a_mat, p_mat, pt_mat = [], [], []
    for h in heads:
        fall = decay(h)
        scaled = fall * rk_r[h]
        a_mat.append(jnp.where(strict, gram[h][:C, :C] * scaled * (b_c[h] * rk_c[h]), 0.0))
        p_mat.append(gram[h][C:, :C] * scaled * rq_c[h])
        pt_mat.append(gram[h][:C, C:] * (decay_t(h) * rq_r[h]) * rk_c[h])

    same16 = (row // 16) == (col // 16)
    same64 = (row // 64) == (col // 64)
    power, inv = [], []
    for h in heads:
        a16 = jnp.where(same16, a_mat[h], 0.0)
        inv.append(eye - a16)
        power.append(fold(mm(wide(a16), right(a16))))
    for level in range(2):
        for h in heads:
            both = fold(mm(jnp.concatenate([wide(inv[h]), wide(power[h])], axis=0), right(power[h])))
            inv[h] = inv[h] + both[:C]
            power[h] = both[C:]
    for h in heads:
        inv[h] = inv[h] + fold(mm(wide(inv[h]), right(power[h])))
    step_mat = []
    for h in heads:
        off = jnp.where(same64, jnp.where(same16, 0.0, a_mat[h]), 0.0)
        step_mat.append(fold(mm(wide(inv[h]), right(off))))
    square = []
    for h in heads:
        both = mm(wide(step_mat[h]), jnp.concatenate([right(inv[h]), right(step_mat[h])], axis=1))
        inv[h] = inv[h] - fold(both[:, :2 * C])
        square.append(fold(both[:, 2 * C:]))
    for h in heads:
        inv[h] = inv[h] + fold(mm(wide(square[h]), right(inv[h])))
    for h in heads:
        off = jnp.where(same64, 0.0, a_mat[h])
        step_mat[h] = fold(mm(wide(inv[h]), right(off)))
    for h in heads:
        inv[h] = inv[h] - fold(mm(wide(step_mat[h]), right(inv[h])))

    u_mat, w_mat = [], []
    for h in heads:
        key, value = part(k_ref, h), part(v_ref, h)
        u_mat.append(mm(wide(inv[h] * b_r[h]), tall2(value)))
        w_mat.append(mm(wide(inv[h] * (b_r[h] * grow_r[h] * rk_r[h])), tall2(key)))
    for h in heads:
        scale = end_c[h] * rk_c[h]
        key_t = jnp.transpose(part(k_ref, h))
        tb = mm(key_t, jnp.concatenate([wide(w_mat[h] * scale), wide(u_mat[h] * scale)], axis=1))
        tbc[h, 0] = gamma[h] * eye - fold(tb[:, :2 * D])
        tbc[h, 1] = jnp.transpose(fold(tb[:, 2 * D:]))
    for h in heads:
        pwu = mm(wide(p_mat[h]), jnp.concatenate([right(w_mat[h]), right(u_mat[h])], axis=1))
        keep_pu[h] = fold(pwu[:, 2 * D:])
        keep_u[h] = u_mat[h]
        e1 = part(q_ref, h).astype(f32) * (rq_c[h] * grow_c[h]) - fold(pwu[:, :2 * D])
        keep_ew[h, :C] = wide(e1)
        keep_ew[h, C:] = wide(w_mat[h])
        tbc[h, 2] = fold(mm(jnp.transpose(part(do_ref, h)), wide(e1)))

    pl.semaphore_wait(barrier, nseq - 1 + nx - 1 + nz - 1)

    def swap(hh):
        return pltpu.make_async_remote_copy(
            src_ref=tbc.at[2 * other + hh], dst_ref=exch.at[hh],
            send_sem=exch_send.at[hh], recv_sem=exch_recv.at[hh],
            device_id={"c": other}, device_id_type=MESH,
        )

    for hh in range(2):
        swap(hh).start()

    for h in heads:
        z = mm(wide(pt_mat[h]), tall2(part(do_ref, h)))
        inv_t = wide(jnp.transpose(inv[h]))
        key_end = part(k_ref, h).astype(f32) * (end_c[h] * rk_c[h])
        both = mm(inv_t, jnp.concatenate([right(z), right(key_end)], axis=1))
        keep_y0[h] = fold(both[:, :2 * D])
        keep_f1[h] = wide(fold(both[:, 2 * D:]))

    first = c == 0
    for hh in range(2):
        swap(hh).wait()

    def pair(hh, item):
        mine, theirs = tbc[2 * c + hh, item], exch[hh, item]
        return jnp.where(first, mine, theirs), jnp.where(first, theirs, mine)

    for hh in range(2):
        t0, t1 = pair(hh, 0)
        b0, b1 = pair(hh, 1)
        c0, c1 = pair(hh, 2)
        both = fold(mm(jnp.concatenate([wide(t1), wide(c1)], axis=0), right(t0)))
        whole = both[:D]
        chip_t[hh] = right(whole)
        chip_tt[hh] = right_t(whole)
        chip_b[hh] = fold(mm_t(wide(b0), right_t(t1))) + b1
        chip_c[hh] = both[D:] + c0

    chunks = [(hh, r) for hh in range(2) for r in range(0, D, ROWS)]
    per_head = D // ROWS

    def f_copy(i, source):
        hh, r = chunks[i]
        return pltpu.make_async_remote_copy(
            src_ref=source.at[hh, pl.ds(r, ROWS)], dst_ref=fin.at[hh, pl.ds(r, ROWS)],
            send_sem=f_send.at[i], recv_sem=f_recv.at[i],
            device_id={"y": lax.rem(y + 1, ny)}, device_id_type=MESH,
        )

    def b_copy(i, source):
        hh, r = chunks[i]
        return pltpu.make_async_remote_copy(
            src_ref=source.at[hh, pl.ds(r, ROWS)], dst_ref=bin_.at[hh, pl.ds(r, ROWS)],
            send_sem=b_send.at[i], recv_sem=b_recv.at[i],
            device_id={"y": lax.rem(y + ny - 1, ny)}, device_id_type=MESH,
        )

    def s_copy(hh):
        return pltpu.make_async_remote_copy(
            src_ref=sends.at[hh], dst_ref=s0.at[2 * c + hh],
            send_sem=s_send.at[hh], recv_sem=s_recv.at[hh],
            device_id={"c": other}, device_id_type=MESH,
        )

    def d_copy(hh):
        return pltpu.make_async_remote_copy(
            src_ref=sendd.at[hh], dst_ref=ds1.at[2 * c + hh],
            send_sem=d_send.at[hh], recv_sem=d_recv.at[hh],
            device_id={"c": other}, device_id_type=MESH,
        )

    @pl.when(y == 0)
    def _():
        for i in range(len(chunks)):
            f_copy(i, chip_b).start()

    @pl.when(y == ny - 1)
    def _():
        for i in range(len(chunks)):
            b_copy(i, chip_c).start()

    for h in heads:
        between = g_c[h] - g_r[h]
        keep_pa[h, :C] = wide(jnp.where(lower, p_mat[h] * between, 0.0))
        keep_pa[h, C:] = wide(jnp.where(strict, a_mat[h] * between, 0.0))

    def last_forward(hh):
        t0, _ = pair(hh, 0)
        b0, _ = pair(hh, 1)
        start = fin[hh]
        middle = fold(mm_t(wide(start), right_t(t0))) + b0
        s0[2 * c + hh] = jnp.where(first, start, middle)
        sends[hh] = jnp.where(first, middle, start)
        s_copy(hh).start()

    def last_backward(hh):
        _, t1 = pair(hh, 0)
        _, c1 = pair(hh, 2)
        end = bin_[hh]
        middle = fold(mm(wide(end), right(t1))) + c1
        ds1[2 * c + hh] = jnp.where(first, middle, end)
        sendd[hh] = jnp.where(first, end, middle)
        d_copy(hh).start()

    def forward():
        @pl.when(y == 0)
        def _():
            fin[...] = jnp.zeros_like(fin)

        @pl.when(jnp.logical_and(y > 0, y < ny - 1))
        def _():
            for i, (hh, r) in enumerate(chunks):
                here = pl.ds(r, ROWS)
                f_copy(i, fout).wait_recv()
                fout[hh, here] = fold(mm_t(wide(fin[hh, here]), chip_tt[hh])) + chip_b[hh, here]
                f_copy(i, fout).start()

        for hh in range(2):
            @pl.when(y == ny - 1)
            def _():
                for i in range(hh * per_head, (hh + 1) * per_head):
                    f_copy(i, fout).wait_recv()

            last_forward(hh)

    def backward():
        @pl.when(y == ny - 1)
        def _():
            bin_[...] = jnp.zeros_like(bin_)

        @pl.when(jnp.logical_and(y > 0, y < ny - 1))
        def _():
            for i, (hh, r) in enumerate(chunks):
                here = pl.ds(r, ROWS)
                b_copy(i, bout).wait_recv()
                bout[hh, here] = fold(mm(wide(bin_[hh, here]), chip_t[hh])) + chip_c[hh, here]
                b_copy(i, bout).start()

        for hh in range(2):
            @pl.when(y == 0)
            def _():
                for i in range(hh * per_head, (hh + 1) * per_head):
                    b_copy(i, bout).wait_recv()

            last_backward(hh)

    @pl.when(y < ny // 2)
    def _():
        forward()
        backward()

    @pl.when(y >= ny // 2)
    def _():
        backward()
        forward()

    for hh in range(2):
        s_copy(hh).wait()
        d_copy(hh).wait()

    @pl.when(y < ny - 1)
    def _():
        for i in range(len(chunks)):
            f_copy(i, fout).wait_send()

    @pl.when(y > 0)
    def _():
        for i in range(len(chunks)):
            b_copy(i, bout).wait_send()

    groups = (
        (me, nseq, ar_seq, seq_send, seq_recv, lambda p: {"y": p // 2, "c": lax.rem(p, 2)}),
        (ix, nx, ar_x, x_send, x_recv, lambda p: {"x": p}),
        (iz, nz, ar_z, z_send, z_recv, lambda p: {"z": p}),
    )

    def part_copy(slot, step):
        index, count, buf, send, recv, device = groups[slot]
        return pltpu.make_async_remote_copy(
            src_ref=ar_own.at[slot], dst_ref=buf.at[index],
            send_sem=send.at[step], recv_sem=recv.at[step],
            device_id=device(lax.rem(index + step, count)), device_id_type=MESH,
        )

    def sum_start(slot, total):
        index, count, buf = groups[slot][:3]
        ar_own[slot] = total
        for step in range(1, count):
            part_copy(slot, step).start()
        buf[index] = total

    def sum_finish(slot):
        _, count, buf = groups[slot][:3]
        for step in range(1, count):
            part_copy(slot, step).wait()
        result = buf[0]
        for j in range(1, count):
            result = result + buf[j]
        return result

    d_mat, y_mat, dds_mat, dot_s, rate_rows = [], [], [], [], []
    for h in heads:
        start, end = s0[h], ds1[h]
        ew = fold(mm_t(keep_ew[h], right_t(start)))
        o_ref[:, h * D:(h + 1) * D] = (keep_pu[h] + ew[:C]).astype(bf16)
        d_mat.append(keep_u[h] - ew[C:])
        y_mat.append(keep_y0[h] + fold(mm_t(keep_f1[h], right_t(end))))
        dot_s.append(jnp.sum(start * end, axis=0, keepdims=True))
    for h in heads:
        key, query, cot = part(k_ref, h), part(q_ref, h), part(do_ref, h)
        high, low = split(s0[h])
        raw = fold(mm_t(jnp.concatenate([query, key], axis=0), jnp.concatenate([high, low], axis=0)))
        dm_right = right(d_mat[h])
        scored = fold(mm(keep_pa[h], dm_right))
        dds = fold(mm(wide(d_mat[h]), right(ds1[h]))) * end_c[h]
        dds_mat.append(dds)
        gated = g_c[h] * grow_c[h]
        terms = cot.astype(f32) * (scored[:C] + raw[:C] * (gated * rq_c[h]))
        terms = terms - y_mat[h] * (scored[C:] + raw[C:] * (gated * b_c[h] * rk_c[h]))
        terms = terms + (key.astype(f32) * dds) * ((g_end[h] - g_c[h]) * rk_c[h])
        rate_rows.append(jnp.sum(terms, axis=0, keepdims=True) + (g_end[h] * gamma[h]) * dot_s[h])
    own = jnp.concatenate(rate_rows + [jnp.zeros((8 - H, C), f32)], axis=0)
    sum_start(0, own)

    lane = lax.broadcasted_iota(jnp.int32, (C, C), 1)
    last = lax.broadcasted_iota(jnp.int32, (C, 1), 0) == C - 1

    def gradients(h):
        key, query, value, cot = part(k_ref, h), part(q_ref, h), part(v_ref, h), part(do_ref, h)
        dm, ym, dds = d_mat[h], y_mat[h], dds_mat[h]
        left = jnp.concatenate([jnp.concatenate([cot, jnp.zeros_like(cot)], axis=1), wide(ym)], axis=0)
        with_s = fold(mm(left, right(s0[h])))
        with_d = fold(mm_t(left, right_t(dm)))
        y_high, y_low = split(ym)
        flipped = mm_t(
            wide(dm),
            jnp.concatenate([
                jnp.concatenate([cot, cot], axis=1),
                jnp.concatenate([y_high, y_high], axis=1),
                jnp.concatenate([y_low, y_low], axis=1),
            ], axis=0),
        )
        fall = decay(h) * rk_r[h]
        fall_t = decay_t(h)
        x_w = with_d[:C] * fall
        n_w = jnp.where(strict, with_d[C:] * fall, 0.0) * (-b_c[h])
        xn = mm(jnp.concatenate([wide(x_w), wide(n_w)], axis=0), tall2(key))
        xt = flipped[:, :C] * (fall_t * rq_r[h])
        nt = jnp.where(strict_upper, (flipped[:, C:2 * C] + flipped[:, 2 * C:]) * fall_t, 0.0) * (-b_r[h] * rk_r[h])
        dk_col = mm(jnp.concatenate([wide(nt), wide(xt)], axis=1), jnp.concatenate([tall2(key), tall2(query)], axis=0)) + dds
        dqn = with_s[:C] * grow_c[h] + xn[:C]
        dk_row = xn[C:] - with_s[C:] * (b_c[h] * grow_c[h])
        kn = key.astype(f32) * rk_c[h]
        qn = query.astype(f32) * rq_c[h]
        sum_q = rows_of(qn * dqn)
        sum_r = rows_of(kn * dk_row)
        sum_c = rows_of(kn * dk_col)
        sum_e = jnp.sum(rows_of(kn * dds), axis=0, keepdims=True)
        sum_v = rows_of(ym * value.astype(f32))
        dq_ref[:, h * D:(h + 1) * D] = ((dqn - qn * sum_q) * rq_c[h]).astype(bf16)
        dk_ref[:, h * D:(h + 1) * D] = ((dk_row + dk_col - kn * (sum_r + sum_c)) * rk_c[h]).astype(bf16)
        dv_ref[:, h * D:(h + 1) * D] = (ym * b_c[h]).astype(bf16)
        dbeta = sum_v + sum_r / b_c[h]
        dg = sum_q + sum_r - sum_c + jnp.where(last, sum_e + gamma[h] * rows_of(dot_s[h]), 0.0)
        return dg, dbeta

    gathered = jnp.zeros((C, C), f32)

    def place(gathered, h):
        dg, dbeta = gradients(h)
        gathered = jnp.where(lane == h, dg, gathered)
        return jnp.where(lane == H + h, dbeta, gathered)

    for h in range(H // 2):
        gathered = place(gathered, h)
    sum_start(1, sum_finish(0))
    for h in range(H // 2, H):
        gathered = place(gathered, h)
    sum_start(2, sum_finish(1))
    as_rows = jnp.transpose(gathered)
    dbeta_ref[...] = as_rows[H:2 * H]
    tri_low = jnp.where(lower, 1.0, 0.0).astype(bf16)
    back = mm(jnp.concatenate(split3(as_rows[:H]), axis=0), tri_low)
    dlog = back[:H] + back[H:2 * H] + back[2 * H:]
    dalpha_ref[...] = dlog * -rate * jax.nn.sigmoid(alpha)
    total = sum_finish(2)
    for h in heads:
        drate_ref[h] = jnp.sum(total[h:h + 1, :])


def deliver(*refs):
    count = 6
    ins, rate_in, outs, rate_out, sem = refs[:count], refs[count], refs[count + 1:2 * count + 1], refs[-2], refs[-1]
    copies = [pltpu.make_async_copy(ins[i], outs[i], sem.at[i]) for i in range(count)]
    for copy in copies:
        copy.start()
    for h in range(H):
        rate_out[h] = rate_in[h]
    for copy in copies:
        copy.wait()


def local(sizes, queries, keys, values, alpha, beta, log_rate, grad_out):
    ny, nx, nz = sizes
    vmem = pl.BlockSpec(memory_space=pltpu.VMEM)
    smem = pl.BlockSpec(memory_space=pltpu.SMEM)
    wide_out = jax.ShapeDtypeStruct((C, H * D), bf16)
    gate_out = jax.ShapeDtypeStruct((H, C), f32)
    chunk_count = 2 * (D // ROWS)
    dma = pltpu.SemaphoreType.DMA
    square = (D, D)
    shapes = (wide_out, wide_out, wide_out, wide_out, gate_out, gate_out, jax.ShapeDtypeStruct((H,), f32))
    outs = pl.pallas_call(
        functools.partial(kernel, sizes),
        name="delta_rule",
        out_shape=shapes,
        in_specs=[vmem, vmem, vmem, vmem, vmem, smem, vmem],
        out_specs=(vmem, vmem, vmem, vmem, vmem, vmem, smem),
        scratch_shapes=[
            pltpu.VMEM((H, 3) + square, f32),
            pltpu.VMEM((2, 3) + square, f32),
            pltpu.VMEM((2, 2 * D, 2 * D), bf16),
            pltpu.VMEM((2, 2 * D, 2 * D), bf16),
            pltpu.VMEM((2,) + square, f32),
            pltpu.VMEM((2,) + square, f32),
            pltpu.VMEM((2,) + square, f32),
            pltpu.VMEM((2,) + square, f32),
            pltpu.VMEM((2,) + square, f32),
            pltpu.VMEM((2,) + square, f32),
            pltpu.VMEM((2,) + square, f32),
            pltpu.VMEM((2,) + square, f32),
            pltpu.VMEM((H,) + square, f32),
            pltpu.VMEM((H,) + square, f32),
            pltpu.VMEM((H,) + square, f32),
            pltpu.VMEM((H,) + square, f32),
            pltpu.VMEM((H,) + square, f32),
            pltpu.VMEM((H, 2 * C, 2 * D), bf16),
            pltpu.VMEM((H, C, 2 * D), bf16),
            pltpu.VMEM((H, 2 * C, 2 * C), bf16),
            pltpu.VMEM((2 * ny, 8, C), f32),
            pltpu.VMEM((nx, 8, C), f32),
            pltpu.VMEM((nz, 8, C), f32),
            pltpu.VMEM((3, 8, C), f32),
            dma((2,)), dma((2,)),
            dma((chunk_count,)), dma((chunk_count,)),
            dma((chunk_count,)), dma((chunk_count,)),
            dma((2,)), dma((2,)), dma((2,)), dma((2,)),
            dma((2 * ny,)), dma((2 * ny,)),
            dma((nx,)), dma((nx,)), dma((nz,)), dma((nz,)),
        ],
        compiler_params=pltpu.CompilerParams(collective_id=0, has_side_effects=True),
    )(
        queries[0], keys[0], values[0],
        jnp.swapaxes(alpha[0], 0, 1), jnp.swapaxes(beta[0], 0, 1), log_rate, grad_out[0],
    )
    outs = pl.pallas_call(
        deliver,
        name="deliver",
        out_shape=shapes,
        in_specs=[vmem] * 6 + [smem],
        out_specs=tuple([pl.BlockSpec(memory_space=pl.ANY)] * 6 + [smem]),
        scratch_shapes=[dma((6,))],
    )(*outs)
    return (
        outs[0][None], outs[1][None], outs[2][None], outs[3][None],
        jnp.swapaxes(outs[4], 0, 1)[None], jnp.swapaxes(outs[5], 0, 1)[None], outs[6],
    )


def build(devices, ny, nx, nz):
    axes = Mesh(devices.reshape(ny, 2, nx, nz), ("y", "c", "x", "z"))
    rows = P(("x", "z"), ("y", "c"), None)
    return jax.shard_map(
        functools.partial(local, (ny, nx, nz)),
        mesh=axes,
        in_specs=(rows, rows, rows, rows, rows, P(), rows),
        out_specs=(rows, rows, rows, rows, rows, rows, P()),
        check_vma=False,
    )


def solution(mesh):
    return build(mesh.devices, 8, 8, 8)
```

```python
import functools

import jax
import jax.numpy as jnp
from jax import lax
from jax.experimental import pallas as pl
from jax.experimental.pallas import tpu as pltpu
from jax.sharding import Mesh
from jax.sharding import PartitionSpec as P

H = 4
D = 128
C = 128
EPSILON = 1e-06
ROWS = 32
MESH = pl.DeviceIdType.MESH
f32 = jnp.float32
bf16 = jnp.bfloat16


def mm(a, b):
    return lax.dot_general(a, b, (((1,), (0,)), ((), ())), preferred_element_type=f32)


def mm_t(a, b):
    return lax.dot_general(a, b, (((1,), (1,)), ((), ())), preferred_element_type=f32)


def split(x):
    high = x.astype(bf16)
    return high, (x - high.astype(f32)).astype(bf16)


def split3(x):
    high, rest = x.astype(bf16), None
    rest = x - high.astype(f32)
    mid = rest.astype(bf16)
    return high, mid, (rest - mid.astype(f32)).astype(bf16)


def wide(x):
    return jnp.concatenate(split(x), axis=1)


def tall2(x):
    return jnp.concatenate([x, x], axis=0)


def fold(x):
    half = x.shape[1] // 2
    return x[:, :half] + x[:, half:]


def right(b):
    return tall2(wide(b))


def right_t(b):
    high, low = split(b)
    return jnp.concatenate(
        [jnp.concatenate([high, high], axis=1), jnp.concatenate([low, low], axis=1)], axis=0
    )


def rows_of(x):
    return jnp.sum(x, axis=1, keepdims=True)


def kernel(
    sizes,
    q_ref, k_ref, v_ref, alpha_ref, beta_ref, rate_ref, do_ref,
    o_ref, dq_ref, dk_ref, dv_ref, dalpha_ref, dbeta_ref, drate_ref,
    tbc, exch, chip_t, chip_tt, chip_b, chip_c,
    fin, fout, bin_, bout, sends, sendd, s0, ds1,
    keep_u, keep_pu, keep_y0, keep_ew, keep_f1, keep_pa,
    ar_seq, ar_x, ar_z, ar_own,
    exch_send, exch_recv, f_send, f_recv, b_send, b_recv, s_send, s_recv, d_send, d_recv,
    seq_send, seq_recv, x_send, x_recv, z_send, z_recv,
):
    ny, nx, nz = sizes
    y = lax.axis_index("y")
    c = lax.axis_index("c")
    ix = lax.axis_index("x")
    iz = lax.axis_index("z")
    nseq = 2 * ny
    me = 2 * y + c
    other = 1 - c

    barrier = pltpu.get_barrier_semaphore()
    for step in range(1, nseq):
        peer = lax.rem(me + step, nseq)
        pl.semaphore_signal(barrier, inc=1, device_id={"y": peer // 2, "c": lax.rem(peer, 2)}, device_id_type=MESH)
    for step in range(1, nx):
        pl.semaphore_signal(barrier, inc=1, device_id={"x": lax.rem(ix + step, nx)}, device_id_type=MESH)
    for step in range(1, nz):
        pl.semaphore_signal(barrier, inc=1, device_id={"z": lax.rem(iz + step, nz)}, device_id_type=MESH)

    heads = range(H)
    row = lax.broadcasted_iota(jnp.int32, (C, C), 0)
    col = lax.broadcasted_iota(jnp.int32, (C, C), 1)
    lower = row >= col
    strict = row > col
    upper = row <= col
    strict_upper = row < col
    eye = jnp.where(row == col, 1.0, 0.0).astype(f32)

    def part(ref, h):
        return ref[:, h * D:(h + 1) * D]

    alpha = alpha_ref[...]
    beta = beta_ref[...]
    head_row = lax.broadcasted_iota(jnp.int32, (H, C), 0)
    rate = jnp.zeros((H, C), f32)
    for h in heads:
        rate = jnp.where(head_row == h, rate_ref[h], rate)
    rate = jnp.exp(rate)
    soft = jnp.maximum(alpha, 0.0) + jnp.log1p(jnp.exp(-jnp.abs(alpha)))
    log_gate = -rate * soft
    bounded = jnp.maximum(log_gate, -120.0)
    tri_up = jnp.where(upper, 1.0, 0.0).astype(bf16)
    summed = mm(jnp.concatenate(split3(bounded), axis=0), tri_up)
    g_rows = summed[:H] + summed[H:2 * H] + summed[2 * H:]
    stacked = jnp.concatenate([g_rows, beta], axis=0)
    columns = jnp.transpose(jnp.concatenate([stacked, jnp.zeros((C - 2 * H, C), f32)], axis=0))

    g_r = [g_rows[h:h + 1, :] for h in heads]
    b_r = [beta[h:h + 1, :] for h in heads]
    g_c = [columns[:, h:h + 1] for h in heads]
    b_c = [columns[:, H + h:H + h + 1] for h in heads]
    g_end = [g_rows[h:h + 1, C - 1:C] for h in heads]
    gamma = [jnp.exp(g_end[h]) for h in heads]
    grow_c = [jnp.exp(g_c[h]) for h in heads]
    grow_r = [jnp.exp(g_r[h]) for h in heads]
    end_c = [jnp.exp(g_end[h] - g_c[h]) for h in heads]

    gram = []
    for h in heads:
        both = jnp.concatenate([part(k_ref, h), part(q_ref, h)], axis=0)
        gram.append(mm_t(both, both))
    rk_c, rk_r, rq_c, rq_r = [], [], [], []
    for h in heads:
        kk = gram[h][:C, :C] * eye
        qq = gram[h][C:, C:] * eye
        rk_c.append(lax.rsqrt(rows_of(kk) + EPSILON))
        rk_r.append(lax.rsqrt(jnp.sum(kk, axis=0, keepdims=True) + EPSILON))
        rq_c.append(lax.rsqrt(rows_of(qq) + EPSILON))
        rq_r.append(lax.rsqrt(jnp.sum(qq, axis=0, keepdims=True) + EPSILON))

    def decay(h):
        return jnp.exp(jnp.where(lower, g_c[h] - g_r[h], -1e30))

    def decay_t(h):
        return jnp.exp(jnp.where(upper, g_r[h] - g_c[h], -1e30))

    a_mat, p_mat = [], []
    for h in heads:
        fall = decay(h)
        scaled = fall * rk_r[h]
        a_mat.append(jnp.where(strict, gram[h][:C, :C] * scaled * (b_c[h] * rk_c[h]), 0.0))
        p_mat.append(gram[h][C:, :C] * scaled * rq_c[h])

    same16 = (row // 16) == (col // 16)
    same64 = (row // 64) == (col // 64)
    power, inv = [], []
    for h in heads:
        a16 = jnp.where(same16, a_mat[h], 0.0)
        inv.append(eye - a16)
        power.append(fold(mm(wide(a16), right(a16))))
    for level in range(2):
        for h in heads:
            both = fold(mm(jnp.concatenate([wide(inv[h]), wide(power[h])], axis=0), right(power[h])))
            inv[h] = inv[h] + both[:C]
            power[h] = both[C:]
    for h in heads:
        inv[h] = inv[h] + fold(mm(wide(inv[h]), right(power[h])))
    step_mat = []
    for h in heads:
        off = jnp.where(same64, jnp.where(same16, 0.0, a_mat[h]), 0.0)
        step_mat.append(fold(mm(wide(inv[h]), right(off))))
    square = []
    for h in heads:
        both = mm(wide(step_mat[h]), jnp.concatenate([right(inv[h]), right(step_mat[h])], axis=1))
        inv[h] = inv[h] - fold(both[:, :2 * C])
        square.append(fold(both[:, 2 * C:]))
    for h in heads:
        inv[h] = inv[h] + fold(mm(wide(square[h]), right(inv[h])))
    for h in heads:
        off = jnp.where(same64, 0.0, a_mat[h])
        step_mat[h] = fold(mm(wide(inv[h]), right(off)))
    for h in heads:
        inv[h] = inv[h] - fold(mm(wide(step_mat[h]), right(inv[h])))

    u_mat, w_mat = [], []
    for h in heads:
        key, value = part(k_ref, h), part(v_ref, h)
        u_mat.append(mm(wide(inv[h] * b_r[h]), tall2(value)))
        w_mat.append(mm(wide(inv[h] * (b_r[h] * grow_r[h] * rk_r[h])), tall2(key)))
    for h in heads:
        scale = end_c[h] * rk_c[h]
        key_t = jnp.transpose(part(k_ref, h))
        tb = mm(key_t, jnp.concatenate([wide(w_mat[h] * scale), wide(u_mat[h] * scale)], axis=1))
        tbc[h, 0] = gamma[h] * eye - fold(tb[:, :2 * D])
        tbc[h, 1] = jnp.transpose(fold(tb[:, 2 * D:]))
    for h in heads:
        pw = fold(mm(wide(p_mat[h]), right(w_mat[h])))
        e1 = part(q_ref, h).astype(f32) * (rq_c[h] * grow_c[h]) - pw
        keep_ew[h, :C] = wide(e1)
        keep_ew[h, C:] = wide(w_mat[h])
        tbc[h, 2] = fold(mm(jnp.transpose(part(do_ref, h)), wide(e1)))

    pl.semaphore_wait(barrier, nseq - 1 + nx - 1 + nz - 1)

    def swap(hh):
        return pltpu.make_async_remote_copy(
            src_ref=tbc.at[2 * other + hh], dst_ref=exch.at[hh],
            send_sem=exch_send.at[0], recv_sem=exch_recv.at[hh],
            device_id={"c": other}, device_id_type=MESH,
        )

    for hh in range(2):
        swap(hh).start()

    for h in heads:
        keep_u[h] = u_mat[h]
        keep_pu[h] = fold(mm(wide(p_mat[h]), right(u_mat[h])))
        pt_mat = gram[h][:C, C:] * (decay_t(h) * rq_r[h]) * rk_c[h]
        z = mm(wide(pt_mat), tall2(part(do_ref, h)))
        inv_t = wide(jnp.transpose(inv[h]))
        key_end = part(k_ref, h).astype(f32) * (end_c[h] * rk_c[h])
        both = mm(inv_t, jnp.concatenate([right(z), right(key_end)], axis=1))
        keep_y0[h] = fold(both[:, :2 * D])
        keep_f1[h] = wide(fold(both[:, 2 * D:]))

    first = c == 0
    chunks = [(hh, r) for hh in range(2) for r in range(0, D, ROWS)]
    per_head = D // ROWS

    def f_copy(i, source):
        hh, r = chunks[i]
        return pltpu.make_async_remote_copy(
            src_ref=source.at[hh, pl.ds(r, ROWS)], dst_ref=fin.at[hh, pl.ds(r, ROWS)],
            send_sem=f_send.at[0], recv_sem=f_recv.at[i],
            device_id={"y": lax.rem(y + 1, ny)}, device_id_type=MESH,
        )

    def b_copy(i, source):
        hh, r = chunks[i]
        return pltpu.make_async_remote_copy(
            src_ref=source.at[hh, pl.ds(r, ROWS)], dst_ref=bin_.at[hh, pl.ds(r, ROWS)],
            send_sem=b_send.at[0], recv_sem=b_recv.at[i],
            device_id={"y": lax.rem(y + ny - 1, ny)}, device_id_type=MESH,
        )

    def s_copy(hh):
        return pltpu.make_async_remote_copy(
            src_ref=sends.at[hh], dst_ref=s0.at[2 * c + hh],
            send_sem=s_send.at[0], recv_sem=s_recv.at[0],
            device_id={"c": other}, device_id_type=MESH,
        )

    def d_copy(hh):
        return pltpu.make_async_remote_copy(
            src_ref=sendd.at[hh], dst_ref=ds1.at[2 * c + hh],
            send_sem=d_send.at[0], recv_sem=d_recv.at[0],
            device_id={"c": other}, device_id_type=MESH,
        )

    first = c == 0

    def pair(hh, item):
        mine, theirs = tbc[2 * c + hh, item], exch[hh, item]
        return jnp.where(first, mine, theirs), jnp.where(first, theirs, mine)

    for hh in range(2):
        swap(hh).wait_recv()
        t0, t1 = pair(hh, 0)
        b0, b1 = pair(hh, 1)
        c0, c1 = pair(hh, 2)
        both = fold(mm(jnp.concatenate([wide(t1), wide(c1)], axis=0), right(t0)))
        whole = both[:D]
        chip_b[hh] = fold(mm_t(wide(b0), right_t(t1))) + b1
        chip_c[hh] = both[D:] + c0

        @pl.when(y == 0)
        def _():
            for i in range(hh * per_head, (hh + 1) * per_head):
                f_copy(i, chip_b).start()

        @pl.when(y == ny - 1)
        def _():
            for i in range(hh * per_head, (hh + 1) * per_head):
                b_copy(i, chip_c).start()

        chip_t[hh] = right(whole)
        chip_tt[hh] = right_t(whole)

    for h in heads:
        between = g_c[h] - g_r[h]
        keep_pa[h, :C] = wide(jnp.where(lower, p_mat[h] * between, 0.0))
        keep_pa[h, C:] = wide(jnp.where(strict, a_mat[h] * between, 0.0))

    def last_forward(hh):
        t0, _ = pair(hh, 0)
        b0, _ = pair(hh, 1)
        start = fin[hh]
        middle = fold(mm_t(wide(start), right_t(t0))) + b0
        s0[2 * c + hh] = jnp.where(first, start, middle)
        sends[hh] = jnp.where(first, middle, start)
        s_copy(hh).start()

    def last_backward(hh):
        _, t1 = pair(hh, 0)
        _, c1 = pair(hh, 2)
        end = bin_[hh]
        middle = fold(mm(wide(end), right(t1))) + c1
        ds1[2 * c + hh] = jnp.where(first, middle, end)
        sendd[hh] = jnp.where(first, end, middle)
        d_copy(hh).start()

    def forward():
        @pl.when(y == 0)
        def _():
            fin[...] = jnp.zeros_like(fin)

        @pl.when(jnp.logical_and(y > 0, y < ny - 1))
        def _():
            for i, (hh, r) in enumerate(chunks):
                here = pl.ds(r, ROWS)
                f_copy(i, fout).wait_recv()
                fout[hh, here] = fold(mm_t(wide(fin[hh, here]), chip_tt[hh])) + chip_b[hh, here]
                f_copy(i, fout).start()

        for hh in range(2):
            @pl.when(y == ny - 1)
            def _():
                for i in range(hh * per_head, (hh + 1) * per_head):
                    f_copy(i, fout).wait_recv()

            last_forward(hh)

    def backward():
        @pl.when(y == ny - 1)
        def _():
            bin_[...] = jnp.zeros_like(bin_)

        @pl.when(jnp.logical_and(y > 0, y < ny - 1))
        def _():
            for i, (hh, r) in enumerate(chunks):
                here = pl.ds(r, ROWS)
                b_copy(i, bout).wait_recv()
                bout[hh, here] = fold(mm(wide(bin_[hh, here]), chip_t[hh])) + chip_c[hh, here]
                b_copy(i, bout).start()

        for hh in range(2):
            @pl.when(y == 0)
            def _():
                for i in range(hh * per_head, (hh + 1) * per_head):
                    b_copy(i, bout).wait_recv()

            last_backward(hh)

    @pl.when(y < ny // 2)
    def _():
        forward()
        backward()

    @pl.when(y >= ny // 2)
    def _():
        backward()
        forward()

    def all_sent(source, sem, to):
        return pltpu.make_async_remote_copy(
            src_ref=source, dst_ref=source, send_sem=sem.at[0], recv_sem=sem.at[0],
            device_id=to, device_id_type=MESH,
        )

    def all_came(source, landing, sem):
        return pltpu.make_async_remote_copy(
            src_ref=source, dst_ref=landing, send_sem=sem.at[0], recv_sem=sem.at[0],
            device_id={"c": other}, device_id_type=MESH,
        )

    all_came(sends, s0.at[pl.ds(2 * other, 2)], s_recv).wait_recv()
    all_came(sendd, ds1.at[pl.ds(2 * other, 2)], d_recv).wait_recv()

    groups = (
        (me, nseq, ar_seq, seq_send, seq_recv, lambda p: {"y": p // 2, "c": lax.rem(p, 2)}),
        (ix, nx, ar_x, x_send, x_recv, lambda p: {"x": p}),
        (iz, nz, ar_z, z_send, z_recv, lambda p: {"z": p}),
    )

    def part_copy(slot, step):
        index, count, buf, send, recv, device = groups[slot]
        return pltpu.make_async_remote_copy(
            src_ref=ar_own.at[slot], dst_ref=buf.at[index],
            send_sem=send.at[0], recv_sem=recv.at[0],
            device_id=device(lax.rem(index + step, count)), device_id_type=MESH,
        )

    def sum_start(slot, total):
        index, count, buf = groups[slot][:3]
        ar_own[slot] = total
        for step in range(1, count):
            part_copy(slot, step).start()
        buf[index] = total

    def came(slot):
        index, count, buf, send, recv, device = groups[slot]
        others = buf.at[pl.ds(0, count - 1)]
        return pltpu.make_async_remote_copy(
            src_ref=others, dst_ref=others, send_sem=send.at[0], recv_sem=recv.at[0],
            device_id=device(lax.rem(index + 1, count)), device_id_type=MESH,
        )

    def sum_finish(slot):
        _, count, buf = groups[slot][:3]
        if count > 1:
            came(slot).wait_recv()
        result = buf[0]
        for j in range(1, count):
            result = result + buf[j]
        return result

    d_mat, y_mat, dds_mat, dot_s, rate_rows = [], [], [], [], []
    for h in heads:
        start, end = s0[h], ds1[h]
        ew = fold(mm_t(keep_ew[h], right_t(start)))
        o_ref[:, h * D:(h + 1) * D] = (keep_pu[h] + ew[:C]).astype(bf16)
        d_mat.append(keep_u[h] - ew[C:])
        y_mat.append(keep_y0[h] + fold(mm_t(keep_f1[h], right_t(end))))
        dot_s.append(jnp.sum(start * end, axis=0, keepdims=True))
    for h in heads:
        key, query, cot = part(k_ref, h), part(q_ref, h), part(do_ref, h)
        high, low = split(s0[h])
        raw = fold(mm_t(jnp.concatenate([query, key], axis=0), jnp.concatenate([high, low], axis=0)))
        dm_right = right(d_mat[h])
        scored = fold(mm(keep_pa[h], dm_right))
        dds = fold(mm(wide(d_mat[h]), right(ds1[h]))) * end_c[h]
        dds_mat.append(dds)
        gated = g_c[h] * grow_c[h]
        terms = cot.astype(f32) * (scored[:C] + raw[:C] * (gated * rq_c[h]))
        terms = terms - y_mat[h] * (scored[C:] + raw[C:] * (gated * b_c[h] * rk_c[h]))
        terms = terms + (key.astype(f32) * dds) * ((g_end[h] - g_c[h]) * rk_c[h])
        rate_rows.append(jnp.sum(terms, axis=0, keepdims=True) + (g_end[h] * gamma[h]) * dot_s[h])
    lane_row = lax.broadcasted_iota(jnp.int32, (1, C), 1)
    own = jnp.zeros((1, C), f32)
    for h in heads:
        own = jnp.where(lane_row == h, rows_of(rate_rows[h]), own)
    sum_start(0, own)

    lane = lax.broadcasted_iota(jnp.int32, (C, C), 1)
    last = lax.broadcasted_iota(jnp.int32, (C, 1), 0) == C - 1

    def gradients(h):
        key, query, value, cot = part(k_ref, h), part(q_ref, h), part(v_ref, h), part(do_ref, h)
        dm, ym, dds = d_mat[h], y_mat[h], dds_mat[h]
        left = jnp.concatenate([jnp.concatenate([cot, jnp.zeros_like(cot)], axis=1), wide(ym)], axis=0)
        with_s = fold(mm(left, right(s0[h])))
        with_d = fold(mm_t(left, right_t(dm)))
        y_high, y_low = split(ym)
        flipped = mm_t(
            wide(dm),
            jnp.concatenate([
                jnp.concatenate([cot, cot], axis=1),
                jnp.concatenate([y_high, y_high], axis=1),
                jnp.concatenate([y_low, y_low], axis=1),
            ], axis=0),
        )
        fall = decay(h) * rk_r[h]
        fall_t = decay_t(h)
        x_w = with_d[:C] * fall
        n_w = jnp.where(strict, with_d[C:] * fall, 0.0) * (-b_c[h])
        xn = mm(jnp.concatenate([wide(x_w), wide(n_w)], axis=0), tall2(key))
        xt = flipped[:, :C] * (fall_t * rq_r[h])
        nt = jnp.where(strict_upper, (flipped[:, C:2 * C] + flipped[:, 2 * C:]) * fall_t, 0.0) * (-b_r[h] * rk_r[h])
        dk_col = mm(jnp.concatenate([wide(nt), wide(xt)], axis=1), jnp.concatenate([tall2(key), tall2(query)], axis=0)) + dds
        dqn = with_s[:C] * grow_c[h] + xn[:C]
        dk_row = xn[C:] - with_s[C:] * (b_c[h] * grow_c[h])
        kn = key.astype(f32) * rk_c[h]
        qn = query.astype(f32) * rq_c[h]
        sum_q = rows_of(qn * dqn)
        sum_r = rows_of(kn * dk_row)
        sum_c = rows_of(kn * dk_col)
        sum_e = jnp.sum(rows_of(kn * dds), axis=0, keepdims=True)
        sum_v = rows_of(ym * value.astype(f32))
        dq_ref[:, h * D:(h + 1) * D] = ((dqn - qn * sum_q) * rq_c[h]).astype(bf16)
        dk_ref[:, h * D:(h + 1) * D] = ((dk_row + dk_col - kn * (sum_r + sum_c)) * rk_c[h]).astype(bf16)
        dv_ref[:, h * D:(h + 1) * D] = (ym * b_c[h]).astype(bf16)
        dbeta = sum_v + sum_r / b_c[h]
        dg = sum_q + sum_r - sum_c + jnp.where(last, sum_e + gamma[h] * rows_of(dot_s[h]), 0.0)
        return dg, dbeta

    gathered = jnp.zeros((C, C), f32)

    def place(gathered, h):
        dg, dbeta = gradients(h)
        gathered = jnp.where(lane == h, dg, gathered)
        return jnp.where(lane == H + h, dbeta, gathered)

    for h in range(H // 2):
        gathered = place(gathered, h)
    sum_start(1, sum_finish(0))
    for h in range(H // 2, H):
        gathered = place(gathered, h)
    sum_start(2, sum_finish(1))
    as_rows = jnp.transpose(gathered)
    dbeta_ref[...] = as_rows[H:2 * H]
    tri_low = jnp.where(lower, 1.0, 0.0).astype(bf16)
    back = mm(jnp.concatenate(split3(as_rows[:H]), axis=0), tri_low)
    dlog = back[:H] + back[H:2 * H] + back[2 * H:]
    dalpha_ref[...] = dlog * -rate * jax.nn.sigmoid(alpha)
    total = sum_finish(2)
    for h in heads:
        drate_ref[h] = jnp.sum(jnp.where(lane_row == h, total, 0.0))

    all_sent(tbc.at[pl.ds(0, 2)], exch_send, {"c": other}).wait_send()
    all_sent(sends, s_send, {"c": other}).wait_send()
    all_sent(sendd, d_send, {"c": other}).wait_send()

    @pl.when(y < ny - 1)
    def _():
        all_sent(fout, f_send, {"y": lax.rem(y + 1, ny)}).wait_send()

    @pl.when(y > 0)
    def _():
        all_sent(bout, b_send, {"y": lax.rem(y + ny - 1, ny)}).wait_send()

    for slot in range(3):
        if groups[slot][1] > 1:
            came(slot).wait_send()


def deliver(*refs):
    count = 6
    ins, rate_in, outs, rate_out, sem = refs[:count], refs[count], refs[count + 1:2 * count + 1], refs[-2], refs[-1]
    copies = [pltpu.make_async_copy(ins[i], outs[i], sem.at[i]) for i in range(count)]
    for copy in copies:
        copy.start()
    for h in range(H):
        rate_out[h] = rate_in[h]
    for copy in copies:
        copy.wait()


def local(sizes, queries, keys, values, alpha, beta, log_rate, grad_out):
    ny, nx, nz = sizes
    vmem = pl.BlockSpec(memory_space=pltpu.VMEM)
    smem = pl.BlockSpec(memory_space=pltpu.SMEM)
    wide_out = jax.ShapeDtypeStruct((C, H * D), bf16)
    gate_out = jax.ShapeDtypeStruct((H, C), f32)
    chunk_count = 2 * (D // ROWS)
    dma = pltpu.SemaphoreType.DMA
    square = (D, D)
    shapes = (wide_out, wide_out, wide_out, wide_out, gate_out, gate_out, jax.ShapeDtypeStruct((H,), f32))
    outs = pl.pallas_call(
        functools.partial(kernel, sizes),
        name="delta_rule",
        out_shape=shapes,
        in_specs=[vmem, vmem, vmem, vmem, vmem, smem, vmem],
        out_specs=(vmem, vmem, vmem, vmem, vmem, vmem, smem),
        scratch_shapes=[
            pltpu.VMEM((H, 3) + square, f32),
            pltpu.VMEM((2, 3) + square, f32),
            pltpu.VMEM((2, 2 * D, 2 * D), bf16),
            pltpu.VMEM((2, 2 * D, 2 * D), bf16),
            pltpu.VMEM((2,) + square, f32),
            pltpu.VMEM((2,) + square, f32),
            pltpu.VMEM((2,) + square, f32),
            pltpu.VMEM((2,) + square, f32),
            pltpu.VMEM((2,) + square, f32),
            pltpu.VMEM((2,) + square, f32),
            pltpu.VMEM((2,) + square, f32),
            pltpu.VMEM((2,) + square, f32),
            pltpu.VMEM((H,) + square, f32),
            pltpu.VMEM((H,) + square, f32),
            pltpu.VMEM((H,) + square, f32),
            pltpu.VMEM((H,) + square, f32),
            pltpu.VMEM((H,) + square, f32),
            pltpu.VMEM((H, 2 * C, 2 * D), bf16),
            pltpu.VMEM((H, C, 2 * D), bf16),
            pltpu.VMEM((H, 2 * C, 2 * C), bf16),
            pltpu.VMEM((2 * ny, 1, C), f32),
            pltpu.VMEM((nx, 1, C), f32),
            pltpu.VMEM((nz, 1, C), f32),
            pltpu.VMEM((3, 1, C), f32),
            dma((1,)), dma((2,)),
            dma((1,)), dma((chunk_count,)),
            dma((1,)), dma((chunk_count,)),
            dma((1,)), dma((1,)), dma((1,)), dma((1,)),
            dma((1,)), dma((1,)),
            dma((1,)), dma((1,)), dma((1,)), dma((1,)),
        ],
        compiler_params=pltpu.CompilerParams(collective_id=0, has_side_effects=True),
    )(
        queries[0], keys[0], values[0],
        jnp.swapaxes(alpha[0], 0, 1), jnp.swapaxes(beta[0], 0, 1), log_rate, grad_out[0],
    )
    outs = pl.pallas_call(
        deliver,
        name="deliver",
        out_shape=shapes,
        in_specs=[vmem] * 6 + [smem],
        out_specs=tuple([pl.BlockSpec(memory_space=pl.ANY)] * 6 + [smem]),
        scratch_shapes=[dma((6,))],
    )(*outs)
    return (
        outs[0][None], outs[1][None], outs[2][None], outs[3][None],
        jnp.swapaxes(outs[4], 0, 1)[None], jnp.swapaxes(outs[5], 0, 1)[None], outs[6],
    )


def build(devices, ny, nx, nz):
    axes = Mesh(devices.reshape(ny, 2, nx, nz), ("y", "c", "x", "z"))
    rows = P(("x", "z"), ("y", "c"), None)
    return jax.shard_map(
        functools.partial(local, (ny, nx, nz)),
        mesh=axes,
        in_specs=(rows, rows, rows, rows, rows, P(), rows),
        out_specs=(rows, rows, rows, rows, rows, rows, P()),
        check_vma=False,
    )


def solution(mesh):
    return build(mesh.devices, 8, 8, 8)
```

```python
import functools

import jax
import jax.numpy as jnp
from jax import lax
from jax.experimental import pallas as pl
from jax.experimental.pallas import tpu as pltpu
from jax.sharding import Mesh
from jax.sharding import PartitionSpec as P

H = 4
D = 128
C = 128
EPSILON = 1e-06
ROWS = 32
MESH = pl.DeviceIdType.MESH
f32 = jnp.float32
bf16 = jnp.bfloat16


def mm(a, b):
    return lax.dot_general(a, b, (((1,), (0,)), ((), ())), preferred_element_type=f32)


def mm_t(a, b):
    return lax.dot_general(a, b, (((1,), (1,)), ((), ())), preferred_element_type=f32)


def split(x):
    high = x.astype(bf16)
    return high, (x - high.astype(f32)).astype(bf16)


def split3(x):
    high, rest = x.astype(bf16), None
    rest = x - high.astype(f32)
    mid = rest.astype(bf16)
    return high, mid, (rest - mid.astype(f32)).astype(bf16)


def wide(x):
    return jnp.concatenate(split(x), axis=1)


def tall2(x):
    return jnp.concatenate([x, x], axis=0)


def fold(x):
    half = x.shape[1] // 2
    return x[:, :half] + x[:, half:]


def right(b):
    return tall2(wide(b))


def right_t(b):
    high, low = split(b)
    return jnp.concatenate(
        [jnp.concatenate([high, high], axis=1), jnp.concatenate([low, low], axis=1)], axis=0
    )


def rows_of(x):
    return jnp.sum(x, axis=1, keepdims=True)


def kernel(
    sizes,
    q_ref, k_ref, v_ref, alpha_ref, beta_ref, rate_ref, do_ref,
    o_ref, dq_ref, dk_ref, dv_ref, dalpha_ref, dbeta_ref, drate_ref,
    tbc, exch, chip_t, chip_tt, chip_b, chip_c,
    fin, fout, bin_, bout, sends, sendd, s0, ds1,
    keep_u, keep_pu, keep_y0, keep_ew, keep_f1, keep_pa,
    ar_seq, ar_plane, ar_own,
    exch_send, exch_recv, f_send, f_recv, b_send, b_recv, s_send, s_recv, d_send, d_recv,
    seq_send, seq_recv, plane_send, plane_recv,
):
    ny, nx, nz = sizes
    y = lax.axis_index("y")
    c = lax.axis_index("c")
    ix = lax.axis_index("x")
    iz = lax.axis_index("z")
    nseq = 2 * ny
    me = 2 * y + c
    other = 1 - c

    barrier = pltpu.get_barrier_semaphore()
    for step in range(1, nseq):
        peer = lax.rem(me + step, nseq)
        pl.semaphore_signal(barrier, inc=1, device_id={"y": peer // 2, "c": lax.rem(peer, 2)}, device_id_type=MESH)
    nplane = nx * nz
    spot = ix * nz + iz

    def greet(step, carry):
        peer = lax.rem(spot + step, nplane)
        pl.semaphore_signal(barrier, inc=1, device_id={"x": peer // nz, "z": lax.rem(peer, nz)}, device_id_type=MESH)
        return carry

    lax.fori_loop(1, nplane, greet, 0)

    heads = range(H)
    row = lax.broadcasted_iota(jnp.int32, (C, C), 0)
    col = lax.broadcasted_iota(jnp.int32, (C, C), 1)
    lower = row >= col
    strict = row > col
    upper = row <= col
    strict_upper = row < col
    eye = jnp.where(row == col, 1.0, 0.0).astype(f32)

    def part(ref, h):
        return ref[:, h * D:(h + 1) * D]

    alpha = alpha_ref[...]
    beta = beta_ref[...]
    head_row = lax.broadcasted_iota(jnp.int32, (H, C), 0)
    rate = jnp.zeros((H, C), f32)
    for h in heads:
        rate = jnp.where(head_row == h, rate_ref[h], rate)
    rate = jnp.exp(rate)
    soft = jnp.maximum(alpha, 0.0) + jnp.log1p(jnp.exp(-jnp.abs(alpha)))
    log_gate = -rate * soft
    bounded = jnp.maximum(log_gate, -120.0)
    tri_up = jnp.where(upper, 1.0, 0.0).astype(bf16)
    summed = mm(jnp.concatenate(split3(bounded), axis=0), tri_up)
    g_rows = summed[:H] + summed[H:2 * H] + summed[2 * H:]
    stacked = jnp.concatenate([g_rows, beta], axis=0)
    columns = jnp.transpose(jnp.concatenate([stacked, jnp.zeros((C - 2 * H, C), f32)], axis=0))

    g_r = [g_rows[h:h + 1, :] for h in heads]
    b_r = [beta[h:h + 1, :] for h in heads]
    g_c = [columns[:, h:h + 1] for h in heads]
    b_c = [columns[:, H + h:H + h + 1] for h in heads]
    g_end = [g_rows[h:h + 1, C - 1:C] for h in heads]
    gamma = [jnp.exp(g_end[h]) for h in heads]
    grow_c = [jnp.exp(g_c[h]) for h in heads]
    grow_r = [jnp.exp(g_r[h]) for h in heads]
    end_c = [jnp.exp(g_end[h] - g_c[h]) for h in heads]

    gram = []
    for h in heads:
        both = jnp.concatenate([part(k_ref, h), part(q_ref, h)], axis=0)
        gram.append(mm_t(both, both))
    rk_c, rk_r, rq_c, rq_r = [], [], [], []
    for h in heads:
        kk = gram[h][:C, :C] * eye
        qq = gram[h][C:, C:] * eye
        rk_c.append(lax.rsqrt(rows_of(kk) + EPSILON))
        rk_r.append(lax.rsqrt(jnp.sum(kk, axis=0, keepdims=True) + EPSILON))
        rq_c.append(lax.rsqrt(rows_of(qq) + EPSILON))
        rq_r.append(lax.rsqrt(jnp.sum(qq, axis=0, keepdims=True) + EPSILON))

    def decay(h):
        return jnp.exp(jnp.where(lower, g_c[h] - g_r[h], -1e30))

    def decay_t(h):
        return jnp.exp(jnp.where(upper, g_r[h] - g_c[h], -1e30))

    a_mat, p_mat = [], []
    for h in heads:
        fall = decay(h)
        scaled = fall * rk_r[h]
        a_mat.append(jnp.where(strict, gram[h][:C, :C] * scaled * (b_c[h] * rk_c[h]), 0.0))
        p_mat.append(gram[h][C:, :C] * scaled * rq_c[h])

    same16 = (row // 16) == (col // 16)
    same64 = (row // 64) == (col // 64)
    power, inv = [], []
    for h in heads:
        a16 = jnp.where(same16, a_mat[h], 0.0)
        inv.append(eye - a16)
        power.append(fold(mm(wide(a16), right(a16))))
    for level in range(2):
        for h in heads:
            both = fold(mm(jnp.concatenate([wide(inv[h]), wide(power[h])], axis=0), right(power[h])))
            inv[h] = inv[h] + both[:C]
            power[h] = both[C:]
    for h in heads:
        inv[h] = inv[h] + fold(mm(wide(inv[h]), right(power[h])))
    step_mat = []
    for h in heads:
        off = jnp.where(same64, jnp.where(same16, 0.0, a_mat[h]), 0.0)
        step_mat.append(fold(mm(wide(inv[h]), right(off))))
    square = []
    for h in heads:
        both = mm(wide(step_mat[h]), jnp.concatenate([right(inv[h]), right(step_mat[h])], axis=1))
        inv[h] = inv[h] - fold(both[:, :2 * C])
        square.append(fold(both[:, 2 * C:]))
    for h in heads:
        inv[h] = inv[h] + fold(mm(wide(square[h]), right(inv[h])))
    for h in heads:
        off = jnp.where(same64, 0.0, a_mat[h])
        step_mat[h] = fold(mm(wide(inv[h]), right(off)))
    for h in heads:
        inv[h] = inv[h] - fold(mm(wide(step_mat[h]), right(inv[h])))

    u_mat, w_mat = [], []
    for h in heads:
        key, value = part(k_ref, h), part(v_ref, h)
        u_mat.append(mm(wide(inv[h] * b_r[h]), tall2(value)))
        w_mat.append(mm(wide(inv[h] * (b_r[h] * grow_r[h] * rk_r[h])), tall2(key)))
    for h in heads:
        scale = end_c[h] * rk_c[h]
        key_t = jnp.transpose(part(k_ref, h))
        tb = mm(key_t, jnp.concatenate([wide(w_mat[h] * scale), wide(u_mat[h] * scale)], axis=1))
        tbc[h, 0] = gamma[h] * eye - fold(tb[:, :2 * D])
        tbc[h, 1] = jnp.transpose(fold(tb[:, 2 * D:]))
    for h in heads:
        pw = fold(mm(wide(p_mat[h]), right(w_mat[h])))
        e1 = part(q_ref, h).astype(f32) * (rq_c[h] * grow_c[h]) - pw
        keep_ew[h, :C] = wide(e1)
        keep_ew[h, C:] = wide(w_mat[h])
        tbc[h, 2] = fold(mm(jnp.transpose(part(do_ref, h)), wide(e1)))

    pl.semaphore_wait(barrier, nseq - 1 + nplane - 1)

    def swap(hh):
        return pltpu.make_async_remote_copy(
            src_ref=tbc.at[2 * other + hh], dst_ref=exch.at[hh],
            send_sem=exch_send.at[0], recv_sem=exch_recv.at[hh],
            device_id={"c": other}, device_id_type=MESH,
        )

    for hh in range(2):
        swap(hh).start()

    for h in heads:
        keep_u[h] = u_mat[h]
        keep_pu[h] = fold(mm(wide(p_mat[h]), right(u_mat[h])))
        pt_mat = gram[h][:C, C:] * (decay_t(h) * rq_r[h]) * rk_c[h]
        z = mm(wide(pt_mat), tall2(part(do_ref, h)))
        inv_t = wide(jnp.transpose(inv[h]))
        key_end = part(k_ref, h).astype(f32) * (end_c[h] * rk_c[h])
        both = mm(inv_t, jnp.concatenate([right(z), right(key_end)], axis=1))
        keep_y0[h] = fold(both[:, :2 * D])
        keep_f1[h] = wide(fold(both[:, 2 * D:]))

    first = c == 0
    chunks = [(hh, r) for hh in range(2) for r in range(0, D, ROWS)]
    per_head = D // ROWS

    def f_copy(i, source):
        hh, r = chunks[i]
        return pltpu.make_async_remote_copy(
            src_ref=source.at[hh, pl.ds(r, ROWS)], dst_ref=fin.at[hh, pl.ds(r, ROWS)],
            send_sem=f_send.at[0], recv_sem=f_recv.at[i],
            device_id={"y": lax.rem(y + 1, ny)}, device_id_type=MESH,
        )

    def b_copy(i, source):
        hh, r = chunks[i]
        return pltpu.make_async_remote_copy(
            src_ref=source.at[hh, pl.ds(r, ROWS)], dst_ref=bin_.at[hh, pl.ds(r, ROWS)],
            send_sem=b_send.at[0], recv_sem=b_recv.at[i],
            device_id={"y": lax.rem(y + ny - 1, ny)}, device_id_type=MESH,
        )

    def s_copy(hh):
        return pltpu.make_async_remote_copy(
            src_ref=sends.at[hh], dst_ref=s0.at[2 * c + hh],
            send_sem=s_send.at[0], recv_sem=s_recv.at[0],
            device_id={"c": other}, device_id_type=MESH,
        )

    def d_copy(hh):
        return pltpu.make_async_remote_copy(
            src_ref=sendd.at[hh], dst_ref=ds1.at[2 * c + hh],
            send_sem=d_send.at[0], recv_sem=d_recv.at[0],
            device_id={"c": other}, device_id_type=MESH,
        )

    first = c == 0

    def pair(hh, item):
        mine, theirs = tbc[2 * c + hh, item], exch[hh, item]
        return jnp.where(first, mine, theirs), jnp.where(first, theirs, mine)

    for hh in range(2):
        swap(hh).wait_recv()
        t0, t1 = pair(hh, 0)
        b0, b1 = pair(hh, 1)
        c0, c1 = pair(hh, 2)
        both = fold(mm(jnp.concatenate([wide(t1), wide(c1)], axis=0), right(t0)))
        whole = both[:D]
        chip_b[hh] = fold(mm_t(wide(b0), right_t(t1))) + b1
        chip_c[hh] = both[D:] + c0

        @pl.when(y == 0)
        def _():
            for i in range(hh * per_head, (hh + 1) * per_head):
                f_copy(i, chip_b).start()

        @pl.when(y == ny - 1)
        def _():
            for i in range(hh * per_head, (hh + 1) * per_head):
                b_copy(i, chip_c).start()

        chip_t[hh] = right(whole)
        chip_tt[hh] = right_t(whole)

    for h in heads:
        between = g_c[h] - g_r[h]
        keep_pa[h, :C] = wide(jnp.where(lower, p_mat[h] * between, 0.0))
        keep_pa[h, C:] = wide(jnp.where(strict, a_mat[h] * between, 0.0))

    def last_forward(hh):
        t0, _ = pair(hh, 0)
        b0, _ = pair(hh, 1)
        start = fin[hh]
        middle = fold(mm_t(wide(start), right_t(t0))) + b0
        s0[2 * c + hh] = jnp.where(first, start, middle)
        sends[hh] = jnp.where(first, middle, start)
        s_copy(hh).start()

    def last_backward(hh):
        _, t1 = pair(hh, 0)
        _, c1 = pair(hh, 2)
        end = bin_[hh]
        middle = fold(mm(wide(end), right(t1))) + c1
        ds1[2 * c + hh] = jnp.where(first, middle, end)
        sendd[hh] = jnp.where(first, end, middle)
        d_copy(hh).start()

    def forward():
        @pl.when(y == 0)
        def _():
            fin[...] = jnp.zeros_like(fin)

        @pl.when(jnp.logical_and(y > 0, y < ny - 1))
        def _():
            for i, (hh, r) in enumerate(chunks):
                here = pl.ds(r, ROWS)
                f_copy(i, fout).wait_recv()
                fout[hh, here] = fold(mm_t(wide(fin[hh, here]), chip_tt[hh])) + chip_b[hh, here]
                f_copy(i, fout).start()

        for hh in range(2):
            @pl.when(y == ny - 1)
            def _():
                for i in range(hh * per_head, (hh + 1) * per_head):
                    f_copy(i, fout).wait_recv()

            last_forward(hh)

    def backward():
        @pl.when(y == ny - 1)
        def _():
            bin_[...] = jnp.zeros_like(bin_)

        @pl.when(jnp.logical_and(y > 0, y < ny - 1))
        def _():
            for i, (hh, r) in enumerate(chunks):
                here = pl.ds(r, ROWS)
                b_copy(i, bout).wait_recv()
                bout[hh, here] = fold(mm(wide(bin_[hh, here]), chip_t[hh])) + chip_c[hh, here]
                b_copy(i, bout).start()

        for hh in range(2):
            @pl.when(y == 0)
            def _():
                for i in range(hh * per_head, (hh + 1) * per_head):
                    b_copy(i, bout).wait_recv()

            last_backward(hh)

    @pl.when(y < ny // 2)
    def _():
        forward()
        backward()

    @pl.when(y >= ny // 2)
    def _():
        backward()
        forward()

    def all_sent(source, sem, to):
        return pltpu.make_async_remote_copy(
            src_ref=source, dst_ref=source, send_sem=sem.at[0], recv_sem=sem.at[0],
            device_id=to, device_id_type=MESH,
        )

    def all_came(source, landing, sem):
        return pltpu.make_async_remote_copy(
            src_ref=source, dst_ref=landing, send_sem=sem.at[0], recv_sem=sem.at[0],
            device_id={"c": other}, device_id_type=MESH,
        )

    all_came(sends, s0.at[pl.ds(2 * other, 2)], s_recv).wait_recv()
    all_came(sendd, ds1.at[pl.ds(2 * other, 2)], d_recv).wait_recv()

    groups = (
        (me, nseq, ar_seq, seq_send, seq_recv, lambda p: {"y": p // 2, "c": lax.rem(p, 2)}),
        (spot, nplane, ar_plane, plane_send, plane_recv, lambda p: {"x": p // nz, "z": lax.rem(p, nz)}),
    )

    def part_copy(slot, step):
        index, count, buf, send, recv, device = groups[slot]
        return pltpu.make_async_remote_copy(
            src_ref=ar_own.at[slot], dst_ref=buf.at[index],
            send_sem=send.at[0], recv_sem=recv.at[0],
            device_id=device(lax.rem(index + step, count)), device_id_type=MESH,
        )

    def sum_start(slot, total):
        index, count, buf = groups[slot][:3]
        ar_own[slot] = total

        def start(step, carry):
            part_copy(slot, step).start()
            return carry

        lax.fori_loop(1, count, start, 0)
        buf[index] = total

    def came(slot):
        index, count, buf, send, recv, device = groups[slot]
        others = buf.at[pl.ds(0, count - 1)]
        return pltpu.make_async_remote_copy(
            src_ref=others, dst_ref=others, send_sem=send.at[0], recv_sem=recv.at[0],
            device_id=device(lax.rem(index + 1, count)), device_id_type=MESH,
        )

    def sum_finish(slot):
        _, count, buf = groups[slot][:3]
        if count > 1:
            came(slot).wait_recv()
        return jnp.sum(buf[...], axis=0)

    d_mat, y_mat, dds_mat, dot_s, rate_rows = [], [], [], [], []
    for h in heads:
        start, end = s0[h], ds1[h]
        ew = fold(mm_t(keep_ew[h], right_t(start)))
        o_ref[:, h * D:(h + 1) * D] = (keep_pu[h] + ew[:C]).astype(bf16)
        d_mat.append(keep_u[h] - ew[C:])
        y_mat.append(keep_y0[h] + fold(mm_t(keep_f1[h], right_t(end))))
        dot_s.append(jnp.sum(start * end, axis=0, keepdims=True))
    for h in heads:
        key, query, cot = part(k_ref, h), part(q_ref, h), part(do_ref, h)
        high, low = split(s0[h])
        raw = fold(mm_t(jnp.concatenate([query, key], axis=0), jnp.concatenate([high, low], axis=0)))
        dm_right = right(d_mat[h])
        scored = fold(mm(keep_pa[h], dm_right))
        dds = fold(mm(wide(d_mat[h]), right(ds1[h]))) * end_c[h]
        dds_mat.append(dds)
        gated = g_c[h] * grow_c[h]
        terms = cot.astype(f32) * (scored[:C] + raw[:C] * (gated * rq_c[h]))
        terms = terms - y_mat[h] * (scored[C:] + raw[C:] * (gated * b_c[h] * rk_c[h]))
        terms = terms + (key.astype(f32) * dds) * ((g_end[h] - g_c[h]) * rk_c[h])
        rate_rows.append(jnp.sum(terms, axis=0, keepdims=True) + (g_end[h] * gamma[h]) * dot_s[h])
    lane_row = lax.broadcasted_iota(jnp.int32, (1, C), 1)
    own = jnp.zeros((1, C), f32)
    for h in heads:
        own = jnp.where(lane_row == h, rows_of(rate_rows[h]), own)
    sum_start(0, own)

    lane = lax.broadcasted_iota(jnp.int32, (C, C), 1)
    last = lax.broadcasted_iota(jnp.int32, (C, 1), 0) == C - 1

    def gradients(h):
        key, query, value, cot = part(k_ref, h), part(q_ref, h), part(v_ref, h), part(do_ref, h)
        dm, ym, dds = d_mat[h], y_mat[h], dds_mat[h]
        left = jnp.concatenate([jnp.concatenate([cot, jnp.zeros_like(cot)], axis=1), wide(ym)], axis=0)
        with_s = fold(mm(left, right(s0[h])))
        with_d = fold(mm_t(left, right_t(dm)))
        y_high, y_low = split(ym)
        flipped = mm_t(
            wide(dm),
            jnp.concatenate([
                jnp.concatenate([cot, cot], axis=1),
                jnp.concatenate([y_high, y_high], axis=1),
                jnp.concatenate([y_low, y_low], axis=1),
            ], axis=0),
        )
        fall = decay(h) * rk_r[h]
        fall_t = decay_t(h)
        x_w = with_d[:C] * fall
        n_w = jnp.where(strict, with_d[C:] * fall, 0.0) * (-b_c[h])
        xn = mm(jnp.concatenate([wide(x_w), wide(n_w)], axis=0), tall2(key))
        xt = flipped[:, :C] * (fall_t * rq_r[h])
        nt = jnp.where(strict_upper, (flipped[:, C:2 * C] + flipped[:, 2 * C:]) * fall_t, 0.0) * (-b_r[h] * rk_r[h])
        dk_col = mm(jnp.concatenate([wide(nt), wide(xt)], axis=1), jnp.concatenate([tall2(key), tall2(query)], axis=0)) + dds
        dqn = with_s[:C] * grow_c[h] + xn[:C]
        dk_row = xn[C:] - with_s[C:] * (b_c[h] * grow_c[h])
        kn = key.astype(f32) * rk_c[h]
        qn = query.astype(f32) * rq_c[h]
        sum_q = rows_of(qn * dqn)
        sum_r = rows_of(kn * dk_row)
        sum_c = rows_of(kn * dk_col)
        sum_e = jnp.sum(rows_of(kn * dds), axis=0, keepdims=True)
        sum_v = rows_of(ym * value.astype(f32))
        dq_ref[:, h * D:(h + 1) * D] = ((dqn - qn * sum_q) * rq_c[h]).astype(bf16)
        dk_ref[:, h * D:(h + 1) * D] = ((dk_row + dk_col - kn * (sum_r + sum_c)) * rk_c[h]).astype(bf16)
        dv_ref[:, h * D:(h + 1) * D] = (ym * b_c[h]).astype(bf16)
        dbeta = sum_v + sum_r / b_c[h]
        dg = sum_q + sum_r - sum_c + jnp.where(last, sum_e + gamma[h] * rows_of(dot_s[h]), 0.0)
        return dg, dbeta

    gathered = jnp.zeros((C, C), f32)

    def place(gathered, h):
        dg, dbeta = gradients(h)
        gathered = jnp.where(lane == h, dg, gathered)
        return jnp.where(lane == H + h, dbeta, gathered)

    for h in heads:
        gathered = place(gathered, h)
    sum_start(1, sum_finish(0))
    as_rows = jnp.transpose(gathered)
    dbeta_ref[...] = as_rows[H:2 * H]
    tri_low = jnp.where(lower, 1.0, 0.0).astype(bf16)
    back = mm(jnp.concatenate(split3(as_rows[:H]), axis=0), tri_low)
    dlog = back[:H] + back[H:2 * H] + back[2 * H:]
    dalpha_ref[...] = dlog * -rate * jax.nn.sigmoid(alpha)
    total = sum_finish(1)
    for h in heads:
        drate_ref[h] = jnp.sum(jnp.where(lane_row == h, total, 0.0))

    all_sent(tbc.at[pl.ds(0, 2)], exch_send, {"c": other}).wait_send()
    all_sent(sends, s_send, {"c": other}).wait_send()
    all_sent(sendd, d_send, {"c": other}).wait_send()

    @pl.when(y < ny - 1)
    def _():
        all_sent(fout, f_send, {"y": lax.rem(y + 1, ny)}).wait_send()

    @pl.when(y > 0)
    def _():
        all_sent(bout, b_send, {"y": lax.rem(y + ny - 1, ny)}).wait_send()

    for slot in range(2):
        if groups[slot][1] > 1:
            came(slot).wait_send()


def deliver(*refs):
    count = 6
    ins, rate_in, outs, rate_out, sem = refs[:count], refs[count], refs[count + 1:2 * count + 1], refs[-2], refs[-1]
    copies = [pltpu.make_async_copy(ins[i], outs[i], sem.at[i]) for i in range(count)]
    for copy in copies:
        copy.start()
    for h in range(H):
        rate_out[h] = rate_in[h]
    for copy in copies:
        copy.wait()


def local(sizes, queries, keys, values, alpha, beta, log_rate, grad_out):
    ny, nx, nz = sizes
    vmem = pl.BlockSpec(memory_space=pltpu.VMEM)
    smem = pl.BlockSpec(memory_space=pltpu.SMEM)
    wide_out = jax.ShapeDtypeStruct((C, H * D), bf16)
    gate_out = jax.ShapeDtypeStruct((H, C), f32)
    chunk_count = 2 * (D // ROWS)
    dma = pltpu.SemaphoreType.DMA
    square = (D, D)
    shapes = (wide_out, wide_out, wide_out, wide_out, gate_out, gate_out, jax.ShapeDtypeStruct((H,), f32))
    outs = pl.pallas_call(
        functools.partial(kernel, sizes),
        name="delta_rule",
        out_shape=shapes,
        in_specs=[vmem, vmem, vmem, vmem, vmem, smem, vmem],
        out_specs=(vmem, vmem, vmem, vmem, vmem, vmem, smem),
        scratch_shapes=[
            pltpu.VMEM((H, 3) + square, f32),
            pltpu.VMEM((2, 3) + square, f32),
            pltpu.VMEM((2, 2 * D, 2 * D), bf16),
            pltpu.VMEM((2, 2 * D, 2 * D), bf16),
            pltpu.VMEM((2,) + square, f32),
            pltpu.VMEM((2,) + square, f32),
            pltpu.VMEM((2,) + square, f32),
            pltpu.VMEM((2,) + square, f32),
            pltpu.VMEM((2,) + square, f32),
            pltpu.VMEM((2,) + square, f32),
            pltpu.VMEM((2,) + square, f32),
            pltpu.VMEM((2,) + square, f32),
            pltpu.VMEM((H,) + square, f32),
            pltpu.VMEM((H,) + square, f32),
            pltpu.VMEM((H,) + square, f32),
            pltpu.VMEM((H,) + square, f32),
            pltpu.VMEM((H,) + square, f32),
            pltpu.VMEM((H, 2 * C, 2 * D), bf16),
            pltpu.VMEM((H, C, 2 * D), bf16),
            pltpu.VMEM((H, 2 * C, 2 * C), bf16),
            pltpu.VMEM((2 * ny, 1, C), f32),
            pltpu.VMEM((nx * nz, 1, C), f32),
            pltpu.VMEM((2, 1, C), f32),
            dma((1,)), dma((2,)),
            dma((1,)), dma((chunk_count,)),
            dma((1,)), dma((chunk_count,)),
            dma((1,)), dma((1,)), dma((1,)), dma((1,)),
            dma((1,)), dma((1,)),
            dma((1,)), dma((1,)),
        ],
        compiler_params=pltpu.CompilerParams(collective_id=0, has_side_effects=True),
    )(
        queries[0], keys[0], values[0],
        jnp.swapaxes(alpha[0], 0, 1), jnp.swapaxes(beta[0], 0, 1), log_rate, grad_out[0],
    )
    outs = pl.pallas_call(
        deliver,
        name="deliver",
        out_shape=shapes,
        in_specs=[vmem] * 6 + [smem],
        out_specs=tuple([pl.BlockSpec(memory_space=pl.ANY)] * 6 + [smem]),
        scratch_shapes=[dma((6,))],
    )(*outs)
    return (
        outs[0][None], outs[1][None], outs[2][None], outs[3][None],
        jnp.swapaxes(outs[4], 0, 1)[None], jnp.swapaxes(outs[5], 0, 1)[None], outs[6],
    )


def build(devices, ny, nx, nz):
    axes = Mesh(devices.reshape(ny, 2, nx, nz), ("y", "c", "x", "z"))
    rows = P(("x", "z"), ("y", "c"), None)
    return jax.shard_map(
        functools.partial(local, (ny, nx, nz)),
        mesh=axes,
        in_specs=(rows, rows, rows, rows, rows, P(), rows),
        out_specs=(rows, rows, rows, rows, rows, rows, P()),
        check_vma=False,
    )


def solution(mesh):
    return build(mesh.devices, 8, 8, 8)
```
